256 devices in a mesh: grp: 32 (over x_hi, z, core), dist: 8 (over y, x_lo).
Axes of the slice: x: 4 (x_hi: 2, x_lo: 2; x = x_hi * 2 + x_lo), y: 4, z: 8, core: 2. Of those that a mesh axis runs over, the one named last changes fastest.
Arguments:
- orbitals: bfloat16 [32, 64, 4096], P('grp', 'dist'), may hold values from -6 to 6
- occupations: bfloat16 [32], P('grp'), may hold values from 0.19921875 to 1
Outputs:
- exchange_action: float32 [32, 64, 4096], P('grp', 'dist')
The draws below stay inside these ranges and needn't reach their ends.
All inputs are finite; a program needn't handle non-finite values.
Results may differ from the reference program's by a relative error of at most 0.0003.
Values may be sent and summed in bfloat16 or wider, within the bound.
No kernel may reach another device: no remote copies, remote signals or barrier semaphores. Data moves between devices by JAX's collectives and lax.ppermute only.
A program may use at most 64 MiB of HBM per device.

```python
import math
import jax
import jax.numpy as jnp
from jax import lax

GRID = 64
ORBITALS = 32


def block_levels(own_key, shape, pieces, least, largest):
    level, own = 1.0, jax.random.fold_in(own_key, 6)
    for dim, blocks in pieces:
        steps = jnp.exp(jax.random.uniform(jax.random.fold_in(own, dim), (blocks,), jnp.float32, least / len(pieces), largest / len(pieces)))
        level = level * jnp.repeat(steps, shape[dim] // blocks).reshape([-1 if axis == dim else 1 for axis in range(len(shape))])
    return level


def scatter_about(rng, dims, scale, limit, shards=(), held_as=jnp.bfloat16):
    drawn = jax.random.normal(rng, dims, jnp.float32) * scale
    if len(shards) > 0:
        drawn = block_levels(rng, dims, shards, -0.22, 0.18) * drawn
    return jnp.clip(drawn, min=-limit, max=limit).astype(held_as)


def setup_inputs(seed: int = 0) -> dict:
    keys = jax.random.split(jax.random.key(seed), 3)
    orbitals = scatter_about(keys[0], (ORBITALS, GRID, GRID * GRID), 1.0, 6.0, ((0, 32), (1, 8)))
    occupations = jnp.clip(0.19921875 + 0.80078125 * jax.random.uniform(keys[1], (ORBITALS,), jnp.float32) ** block_levels(keys[1], (ORBITALS,), ((0, 32),), -0.2, 0.2), 0.19921875, 1.0).astype(jnp.bfloat16)
    return dict(orbitals=orbitals, occupations=occupations)


box_length = 7.0


def reference(orbitals, occupations):
    orbital_count = orbitals.shape[0]
    points = GRID
    fields = orbitals.astype(jnp.float32).reshape(orbital_count, points, points, points)
    weights = occupations.astype(jnp.float32)
    position = jnp.arange(points)
    folded = jnp.minimum(position, points - position).astype(jnp.float32)
    halfway = jnp.arange(points // 2 + 1).astype(jnp.float32)
    squares = folded[:, None, None] ** 2 + folded[None, :, None] ** 2 + halfway[None, None, :] ** 2
    scale = (2.0 * math.pi / box_length) ** 2
    kernel = jnp.where(squares > 0.5, 4.0 * math.pi / (scale * jnp.maximum(squares, 1.0)), 0.0)

    def poisson_solve(density):
        spectrum = jnp.fft.rfftn(density, axes=(1, 2, 3))
        return jnp.fft.irfftn(spectrum * kernel, s=(points, points, points), axes=(1, 2, 3))

    def add_distance(offset, summed):
        partner = jnp.roll(fields, -offset, axis=0)
        partner_weight = jnp.roll(weights, -offset)
        potential = poisson_solve(fields * partner)
        toward = potential * partner * partner_weight[:, None, None, None]
        reverse_weight = jnp.logical_and(offset > 0, 2 * offset < orbital_count).astype(jnp.float32)
        backward = potential * fields * (weights * reverse_weight)[:, None, None, None]
        return summed + toward + jnp.roll(backward, offset, axis=0)

    summed = lax.fori_loop(0, orbital_count // 2 + 1, add_distance, jnp.zeros_like(fields))
    return (-summed).reshape(orbital_count, points, points * points)
```

```python
import math

import jax
import jax.numpy as jnp
import numpy as np
from jax import lax
from jax.experimental import pallas as pl
from jax.experimental.pallas import tpu as pltpu
from jax.sharding import PartitionSpec as P
GRID = 64
GF = 8
GM = 8
box_length = 7.0

def split(x):
    hi = x.astype(jnp.bfloat16)
    lo = (x - hi.astype(jnp.float32)).astype(jnp.bfloat16)
    return hi, lo

def tables():
    position = np.arange(GRID)
    angles = (position[:, None] * position[None, :] % GRID) * (2.0 * math.pi / GRID)
    t = np.cos(angles) + np.sin(angles)
    hi = t.astype(jnp.bfloat16)
    lo = (t - hi.astype(np.float64)).astype(jnp.bfloat16)
    hi, lo = jnp.asarray(hi), jnp.asarray(lo)
    left = jnp.concatenate([hi, hi, lo, lo], axis=1)
    zero = jnp.zeros_like(hi)
    two = lambda m: jnp.concatenate([jnp.concatenate([m, zero], 1), jnp.concatenate([zero, m], 1)], 0)
    wide = jnp.concatenate([two(hi), two(lo)], axis=1)
    right = jnp.concatenate([wide, wide], axis=0)
    return left, right

def green_table():
    p = jnp.arange(GRID, dtype=jnp.int32)
    f = jnp.minimum(p, GRID - p)
    sq = (f * f).astype(jnp.float32)
    tot = sq[:, None, None] + sq[None, :, None] + jnp.concatenate([sq, sq])[None, None, :]
    c = box_length**2 / (math.pi * GRID**3)
    return jnp.where(tot > 0.5, c / jnp.maximum(tot, 1.0), 0.0)

def dot(a, b):
    return jnp.dot(a, b, preferred_element_type=jnp.float32)

def along_lanes(x, right):
    hi, lo = split(x)
    y = dot(jnp.concatenate([hi, lo], axis=1), right)
    return y[:, :128] + y[:, 128:]

def along_rows(left, x):
    hi, lo = split(x)
    return dot(left, jnp.concatenate([hi, lo, hi, lo], axis=0))

def solve_kernel(place_ref, row_ref, c0_ref, c1_ref, c2_ref, c3_ref, left_ref, right_ref, green_ref, out_ref, f_ref):
    zp = place_ref[0]
    left = left_ref[...]
    right = right_ref[...]
    low = lax.broadcasted_iota(jnp.int32, (GRID, 128), 1) < 64

    def column(ref, lanes):
        return jnp.concatenate([ref[lax.rem(zp - b + 8, 8), :, lanes] for b in range(8)], axis=0).astype(jnp.float32)

    for pack, (a_ref, b_ref) in enumerate(((c0_ref, c1_ref), (c2_ref, c3_ref))):
        def forward(step, _):
            packed = []
            for i in range(GF):
                yh = step * GF + i
                lanes = pl.ds(pl.multiple_of(yh * 128, 128), 128)
                row = row_ref[:, lanes].astype(jnp.float32)
                d1 = row * column(a_ref, lanes)
                d2 = row * column(b_ref, lanes)
                packed.append(jnp.where(low, d1, pltpu.roll(d2, 64, 1)))
                packed.append(jnp.where(low, pltpu.roll(d1, 64, 1), d2))
            g = along_lanes(jnp.concatenate(packed, axis=0), right)
            h = along_rows(left, jnp.concatenate([g[64 * i:64 * i + 64] for i in range(2 * GF)], axis=1))
            f_ref[pl.ds(pl.multiple_of(step * (128 * GF), 128 * GF), 128 * GF), :] = jnp.concatenate([h[:, 128 * i:128 * i + 128] for i in range(2 * GF)], axis=0)
            return 0
        lax.fori_loop(0, 32 // GF, forward, 0)

        def middle(kk, _):
            kx = kk * GM
            g = jnp.concatenate([f_ref[pl.ds(kx + i, 64, stride=64), :] for i in range(GM)], axis=1)
            h = along_rows(left, g)
            h = h * jnp.concatenate([green_ref[kx + i] for i in range(GM)], axis=1)
            u = along_rows(left, h)
            for i in range(GM):
                f_ref[pl.ds(kx + i, 64, stride=64), :] = u[:, 128 * i:128 * i + 128]
            return 0
        lax.fori_loop(0, 64 // GM, middle, 0)

        occ_a = a_ref[0, :, 4096:4224].astype(jnp.float32)[0:1, :]
        occ_b = b_ref[0, :, 4096:4224].astype(jnp.float32)[0:1, :]

        def backward(step, _):
            h = f_ref[pl.ds(pl.multiple_of(step * (128 * GF), 128 * GF), 128 * GF), :]
            g = along_rows(left, jnp.concatenate([h[64 * i:64 * i + 64] for i in range(2 * GF)], axis=1))
            p = along_lanes(jnp.concatenate([g[:, 128 * i:128 * i + 128] for i in range(2 * GF)], axis=0), right)
            for i in range(GF):
                yh = step * GF + i
                lanes = pl.ds(pl.multiple_of(yh * 128, 128), 128)
                p0, p1 = p[128 * i:128 * i + 64], p[128 * i + 64:128 * i + 128]
                v1 = jnp.where(low, p0, pltpu.roll(p1, 64, 1))
                v2 = jnp.where(low, pltpu.roll(p0, 64, 1), p1)
                term = v1 * (column(a_ref, lanes) * occ_a) + v2 * (column(b_ref, lanes) * occ_b)
                if pack:
                    term = out_ref[:, lanes] + term
                out_ref[:, lanes] = term
            return 0
        lax.fori_loop(0, 32 // GF, backward, 0)

def solve(place, row, c0, c1, c2, c3, left, right, green):
    vm = pl.BlockSpec(memory_space=pltpu.VMEM)
    return pl.pallas_call(
        solve_kernel,
        out_shape=jax.ShapeDtypeStruct((GRID, GRID * GRID), jnp.float32),
        in_specs=[pl.BlockSpec(memory_space=pltpu.SMEM)] + [vm] * 8,
        out_specs=vm,
        scratch_shapes=[pltpu.VMEM((GRID * GRID, 128), jnp.float32)],
        name="solve",
    )(place, row, c0, c1, c2, c3, left, right, green)


AXES = ("grp", "dist")


def device(half, z, core, lane):
    return ((half * 8 + z) * 2 + core) * 8 + lane


def moved(x, rule):
    pairs = [
        (device(h, z, c, l), device(*rule(h, z, c, l)))
        for h in range(2)
        for z in range(8)
        for c in range(2)
        for l in range(8)
    ]
    return lax.ppermute(x, AXES, pairs)


def body(orbitals, occupations):
    mine = orbitals[0]
    copies = jnp.broadcast_to(mine, (8, *mine.shape))
    row = lax.all_to_all(copies, "dist", split_axis=0, concat_axis=0, tiled=True)
    row = row.reshape(GRID, GRID * GRID)
    weight = jnp.broadcast_to(occupations[0], (mine.shape[0], 128))
    slice_out = jnp.concatenate([mine, weight], axis=1)
    pieces = [
        moved(slice_out, lambda h, z, c, l, k=k: (h, (l + k) % 8, c, z)) for k in range(8)
    ]
    col = jnp.stack(pieces)
    core_col = moved(col, lambda h, z, c, l: (h, z, 1 - c, l))
    far_col = moved(col, lambda h, z, c, l: (1 - h, z, c, l))
    far_core_col = moved(far_col, lambda h, z, c, l: (h, z, 1 - c, l))
    place = (lax.axis_index("grp") // 2 % 8).astype(jnp.int32).reshape(1)
    left, right = tables()
    partial = solve(place, row, col, core_col, far_col, far_core_col, left, right, green_table())
    arrived = lax.all_to_all(
        partial.reshape(8, 8, GRID * GRID), "dist", split_axis=0, concat_axis=0, tiled=True
    )
    return -arrived.sum(axis=0)[None]


def solution(mesh):
    in_specs = (P("grp", "dist", None), P("grp"))
    out_specs = P("grp", "dist", None)
    return jax.shard_map(body, mesh=mesh, in_specs=in_specs, out_specs=out_specs, check_vma=False)
```

```python
import functools
import math

import jax
import jax.numpy as jnp
import numpy as np
from jax import lax
from jax.experimental import pallas as pl
from jax.experimental.pallas import tpu as pltpu
from jax.sharding import PartitionSpec as P
GRID = 64
GF = 16
GM = 16
box_length = 7.0

def split(x):
    hi = x.astype(jnp.bfloat16)
    lo = (x - hi.astype(jnp.float32)).astype(jnp.bfloat16)
    return hi, lo

def tables():
    position = np.arange(GRID)
    angles = (position[:, None] * position[None, :] % GRID) * (2.0 * math.pi / GRID)
    t = np.cos(angles) + np.sin(angles)
    hi = t.astype(jnp.bfloat16)
    lo = (t - hi.astype(np.float64)).astype(jnp.bfloat16)
    hi, lo = jnp.asarray(hi), jnp.asarray(lo)
    left = jnp.concatenate([hi, hi, lo, lo], axis=1)
    zero = jnp.zeros_like(hi)
    two = lambda m: jnp.concatenate([jnp.concatenate([m, zero], 1), jnp.concatenate([zero, m], 1)], 0)
    wide = jnp.concatenate([two(hi), two(lo)], axis=1)
    right = jnp.concatenate([wide, wide], axis=0)
    return left, right

def green_table():
    p = jnp.arange(GRID, dtype=jnp.int32)
    f = jnp.minimum(p, GRID - p)
    sq = (f * f).astype(jnp.float32)
    tot = sq[:, None, None] + sq[None, :, None] + jnp.concatenate([sq, sq])[None, None, :]
    c = box_length**2 / (math.pi * GRID**3)
    return jnp.where(tot > 0.5, c / jnp.maximum(tot, 1.0), 0.0)

def dot(a, b):
    return jnp.dot(a, b, preferred_element_type=jnp.float32)

def along_lanes(x, right):
    hi, lo = split(x)
    y = dot(jnp.concatenate([hi, lo], axis=1), right)
    return y[:, :128] + y[:, 128:]

def along_rows(left, x):
    hi, lo = split(x)
    return dot(left, jnp.concatenate([hi, lo, hi, lo], axis=0))

def solve_kernel(first, place_ref, row_ref, a_ref, b_ref, left_ref, right_ref, green_ref, *refs):
    if first:
        out_ref, f_ref = refs
    else:
        sum_ref, out_ref, f_ref = refs
    zp = place_ref[0]
    left = left_ref[...]
    right = right_ref[...]
    low = lax.broadcasted_iota(jnp.int32, (GRID, 128), 1) < 64

    def column(ref, lanes):
        pieces = [ref[lax.rem(zp - b + 8, 8), :, lanes] for b in range(8)]
        return jnp.concatenate(pieces, axis=0).astype(jnp.float32)

    def lanes_of(yh):
        return pl.ds(pl.multiple_of(yh * 128, 128), 128)

    def rows_of(step):
        return pl.ds(pl.multiple_of(step * (128 * GF), 128 * GF), 128 * GF)

    def forward(step, _):
        packed = []
        for i in range(GF):
            lanes = lanes_of(step * GF + i)
            row = row_ref[:, lanes].astype(jnp.float32)
            d1 = row * column(a_ref, lanes)
            d2 = row * column(b_ref, lanes)
            packed.append(jnp.where(low, d1, pltpu.roll(d2, 64, 1)))
            packed.append(jnp.where(low, pltpu.roll(d1, 64, 1), d2))
        g = along_lanes(jnp.concatenate(packed, axis=0), right)
        wide = jnp.concatenate([g[64 * i : 64 * i + 64] for i in range(2 * GF)], axis=1)
        h = along_rows(left, wide)
        tall = jnp.concatenate([h[:, 128 * i : 128 * i + 128] for i in range(2 * GF)], axis=0)
        f_ref[rows_of(step), :] = tall
        return 0

    lax.fori_loop(0, 32 // GF, forward, 0)

    def middle(step, _):
        kx = step * GM
        parts = [f_ref[pl.ds(kx + i, 64, stride=64), :] for i in range(GM)]
        h = along_rows(left, jnp.concatenate(parts, axis=1))
        h = h * jnp.concatenate([green_ref[kx + i] for i in range(GM)], axis=1)
        u = along_rows(left, h)
        for i in range(GM):
            f_ref[pl.ds(kx + i, 64, stride=64), :] = u[:, 128 * i : 128 * i + 128]
        return 0

    lax.fori_loop(0, 64 // GM, middle, 0)

    occ_a = a_ref[0, :, 4096:4224].astype(jnp.float32)[0:1, :]
    occ_b = b_ref[0, :, 4096:4224].astype(jnp.float32)[0:1, :]

    def backward(step, _):
        h = f_ref[rows_of(step), :]
        wide = jnp.concatenate([h[64 * i : 64 * i + 64] for i in range(2 * GF)], axis=1)
        g = along_rows(left, wide)
        tall = jnp.concatenate([g[:, 128 * i : 128 * i + 128] for i in range(2 * GF)], axis=0)
        p = along_lanes(tall, right)
        for i in range(GF):
            lanes = lanes_of(step * GF + i)
            p0, p1 = p[128 * i : 128 * i + 64], p[128 * i + 64 : 128 * i + 128]
            v1 = jnp.where(low, p0, pltpu.roll(p1, 64, 1))
            v2 = jnp.where(low, pltpu.roll(p0, 64, 1), p1)
            term = v1 * (column(a_ref, lanes) * occ_a) + v2 * (column(b_ref, lanes) * occ_b)
            if not first:
                term = sum_ref[:, lanes] + term
            out_ref[:, lanes] = term
        return 0

    lax.fori_loop(0, 32 // GF, backward, 0)


def solve(place, row, a, b, left, right, green, summed=None):
    vm = pl.BlockSpec(memory_space=pltpu.VMEM)
    more = () if summed is None else (summed,)
    return pl.pallas_call(
        functools.partial(solve_kernel, summed is None),
        out_shape=jax.ShapeDtypeStruct((GRID, GRID * GRID), jnp.float32),
        in_specs=[pl.BlockSpec(memory_space=pltpu.SMEM)] + [vm] * (6 + len(more)),
        out_specs=vm,
        scratch_shapes=[pltpu.VMEM((GRID * GRID, 128), jnp.float32)],
        cost_estimate=pl.CostEstimate(flops=10**10, bytes_accessed=10**7, transcendentals=0),
        compiler_params=pltpu.CompilerParams(vmem_limit_bytes=32 * 2**20),
        name="solve",
    )(place, row, a, b, left, right, green, *more)


AXES = ("grp", "dist")


def device(half, z, core, lane):
    return ((half * 8 + z) * 2 + core) * 8 + lane


def moved(x, rule):
    pairs = [
        (device(h, z, c, l), device(*rule(h, z, c, l)))
        for h in range(2)
        for z in range(8)
        for c in range(2)
        for l in range(8)
    ]
    return lax.ppermute(x, AXES, pairs)


def body(orbitals, occupations):
    mine = orbitals[0]
    copies = jnp.broadcast_to(mine, (8, *mine.shape))
    row = lax.all_to_all(copies, "dist", split_axis=0, concat_axis=0, tiled=True)
    row = row.reshape(GRID, GRID * GRID)
    weight = jnp.broadcast_to(occupations[0], (mine.shape[0], 128))
    slice_out = jnp.concatenate([mine, weight], axis=1)
    turned = moved(slice_out, lambda h, z, c, l: (h, l, c, z))
    pieces = [turned] + [
        moved(turned, lambda h, z, c, l, k=k: (h, (z + k) % 8, c, l)) for k in range(1, 8)
    ]
    col = jnp.stack(pieces)
    far_col = moved(col, lambda h, z, c, l: (1 - h, z, c, l))
    core_col = moved(col, lambda h, z, c, l: (h, z, 1 - c, l))
    place = ((lax.axis_index("grp") >> 1) & 7).astype(jnp.int32).reshape(1)
    left, right = tables()
    green = green_table()
    partial = solve(place, row, col, core_col, left, right, green)
    far_col, partial = lax.optimization_barrier((far_col, partial))
    far_core_col = moved(far_col, lambda h, z, c, l: (h, z, 1 - c, l))
    partial = solve(place, row, far_col, far_core_col, left, right, green, partial)
    arrived = lax.all_to_all(
        partial.reshape(8, 8, GRID * GRID), "dist", split_axis=0, concat_axis=0, tiled=True
    )
    return -arrived.sum(axis=0)[None]


def solution(mesh):
    in_specs = (P("grp", "dist", None), P("grp"))
    out_specs = P("grp", "dist", None)
    return jax.shard_map(body, mesh=mesh, in_specs=in_specs, out_specs=out_specs, check_vma=False)
```

```python
import functools
import math

import jax
import jax.numpy as jnp
import numpy as np
from jax import lax
from jax.experimental import pallas as pl
from jax.experimental.pallas import tpu as pltpu
from jax.sharding import PartitionSpec as P

GRID = 64
GF = 16
GM = 16
box_length = 7.0


def split(x):
    hi = x.astype(jnp.bfloat16)
    lo = (x - hi.astype(jnp.float32)).astype(jnp.bfloat16)
    return hi, lo


def tables():
    position = np.arange(GRID)
    angles = (position[:, None] * position[None, :] % GRID) * (2.0 * math.pi / GRID)
    t = np.cos(angles) + np.sin(angles)
    hi = t.astype(jnp.bfloat16)
    lo = (t - hi.astype(np.float64)).astype(jnp.bfloat16)
    hi, lo = jnp.asarray(hi), jnp.asarray(lo)
    left = jnp.concatenate([hi, hi, lo, lo], axis=1)
    zero = jnp.zeros_like(hi)
    two = lambda m: jnp.concatenate([jnp.concatenate([m, zero], 1), jnp.concatenate([zero, m], 1)], 0)
    wide = jnp.concatenate([two(hi), two(lo)], axis=1)
    right = jnp.concatenate([wide, wide], axis=0)
    return left, right


def green_table():
    p = jnp.arange(GRID, dtype=jnp.int32)
    f = jnp.minimum(p, GRID - p)
    sq = (f * f).astype(jnp.float32)
    tot = sq[:, None, None] + sq[None, :, None] + jnp.concatenate([sq, sq])[None, None, :]
    c = box_length**2 / (math.pi * GRID**3)
    return jnp.where(tot > 0.5, c / jnp.maximum(tot, 1.0), 0.0)


def dot(a, b):
    return jnp.dot(a, b, preferred_element_type=jnp.float32)


def along_lanes(x, right):
    hi, lo = split(x)
    y = dot(jnp.concatenate([hi, lo], axis=1), right)
    return y[:, :128] + y[:, 128:]


def along_rows(left, x):
    hi, lo = split(x)
    return dot(left, jnp.concatenate([hi, lo, hi, lo], axis=0))


def solve_kernel(first, place_ref, order_ref, row_ref, a_ref, b_ref, left_ref, right_ref, green_ref, *refs):
    if first:
        out_ref, f_ref = refs
    else:
        sum_ref, out_ref, f_ref = refs
    where = [order_ref[lax.rem(place_ref[0] - b + 8, 8)] for b in range(8)]
    left = left_ref[...]
    right = right_ref[...]
    low = lax.broadcasted_iota(jnp.int32, (GRID, 128), 1) < 64

    def column(ref, lanes):
        pieces = [ref[where[b], :, lanes] for b in range(8)]
        return jnp.concatenate(pieces, axis=0).astype(jnp.float32)

    def lanes_of(yh):
        return pl.ds(pl.multiple_of(yh * 128, 128), 128)

    def rows_of(step):
        return pl.ds(pl.multiple_of(step * (128 * GF), 128 * GF), 128 * GF)

    def forward(step, _):
        packed = []
        for i in range(GF):
            lanes = lanes_of(step * GF + i)
            row = row_ref[:, lanes].astype(jnp.float32)
            d1 = row * column(a_ref, lanes)
            d2 = row * column(b_ref, lanes)
            packed.append(jnp.where(low, d1, pltpu.roll(d2, 64, 1)))
            packed.append(jnp.where(low, pltpu.roll(d1, 64, 1), d2))
        g = along_lanes(jnp.concatenate(packed, axis=0), right)
        wide = jnp.concatenate([g[64 * i : 64 * i + 64] for i in range(2 * GF)], axis=1)
        h = along_rows(left, wide)
        tall = jnp.concatenate([h[:, 128 * i : 128 * i + 128] for i in range(2 * GF)], axis=0)
        f_ref[rows_of(step), :] = tall
        return 0

    lax.fori_loop(0, 32 // GF, forward, 0)

    def middle(step, _):
        kx = step * GM
        parts = [f_ref[pl.ds(kx + i, 64, stride=64), :] for i in range(GM)]
        h = along_rows(left, jnp.concatenate(parts, axis=1))
        h = h * jnp.concatenate([green_ref[kx + i] for i in range(GM)], axis=1)
        u = along_rows(left, h)
        for i in range(GM):
            f_ref[pl.ds(kx + i, 64, stride=64), :] = u[:, 128 * i : 128 * i + 128]
        return 0

    lax.fori_loop(0, 64 // GM, middle, 0)

    occ_a = -a_ref[0, :, 4096:4224].astype(jnp.float32)[0:1, :]
    occ_b = -b_ref[0, :, 4096:4224].astype(jnp.float32)[0:1, :]

    def backward(step, _):
        h = f_ref[rows_of(step), :]
        wide = jnp.concatenate([h[64 * i : 64 * i + 64] for i in range(2 * GF)], axis=1)
        g = along_rows(left, wide)
        tall = jnp.concatenate([g[:, 128 * i : 128 * i + 128] for i in range(2 * GF)], axis=0)
        p = along_lanes(tall, right)
        for i in range(GF):
            lanes = lanes_of(step * GF + i)
            p0, p1 = p[128 * i : 128 * i + 64], p[128 * i + 64 : 128 * i + 128]
            v1 = jnp.where(low, p0, pltpu.roll(p1, 64, 1))
            v2 = jnp.where(low, pltpu.roll(p0, 64, 1), p1)
            term = v1 * (column(a_ref, lanes) * occ_a) + v2 * (column(b_ref, lanes) * occ_b)
            if not first:
                term = sum_ref[:, lanes] + term
            out_ref[:, lanes] = term
        return 0

    lax.fori_loop(0, 32 // GF, backward, 0)
    if not first:
        level = jnp.zeros((GRID, 128), jnp.float32)
        for i in range(32):
            level = jnp.maximum(level, jnp.abs(out_ref[:, 128 * i : 128 * i + 128]))
        peak = jnp.maximum(jnp.max(level, axis=(0, 1), keepdims=True), 1e-30)
        power = jnp.ceil(jnp.log2(jnp.broadcast_to(peak, (8, 128)))) - 15.0
        factor = jnp.exp2(-power)[0:1]
        for i in range(32):
            lanes = slice(128 * i, 128 * i + 128)
            out_ref[:, lanes] = out_ref[:, lanes] * factor
        out_ref[:, 4096:4224] = jnp.broadcast_to(power[0:1], (GRID, 128))


def solve(place, row, a, b, left, right, green, *more):
    vm = pl.BlockSpec(memory_space=pltpu.VMEM)
    sm = pl.BlockSpec(memory_space=pltpu.SMEM)
    order = jnp.asarray(np.argsort(ORDER), jnp.int32)
    width = GRID * GRID + (128 if more else 0)
    return pl.pallas_call(
        functools.partial(solve_kernel, not more),
        out_shape=jax.ShapeDtypeStruct((GRID, width), jnp.float32),
        in_specs=[sm, sm] + [vm] * (6 + len(more)),
        out_specs=vm,
        scratch_shapes=[pltpu.VMEM((GRID * GRID, 128), jnp.float32)],
        cost_estimate=pl.CostEstimate(flops=10**10, bytes_accessed=10**7, transcendentals=0),
        compiler_params=pltpu.CompilerParams(vmem_limit_bytes=32 * 2**20),
        name="solve",
    )(place, order, row, a, b, left, right, green, *more)


AXES = ("grp", "dist")
ORDER = (0, 4, 3, 5, 2, 6, 1, 7)


def device(half, z, core, lane):
    return ((half * 8 + z) * 2 + core) * 8 + lane


def moved(x, rule):
    pairs = [
        (device(h, z, c, l), device(*rule(h, z, c, l)))
        for h in range(2)
        for z in range(8)
        for c in range(2)
        for l in range(8)
    ]
    return lax.ppermute(x, AXES, pairs)


def body(orbitals, occupations):
    return exchange(orbitals[0], occupations[0])


def exchange(mine, occupation):
    slice_out = jnp.concatenate([mine, jnp.broadcast_to(occupation, (8, 128))], axis=1)
    turned = moved(slice_out, lambda h, z, c, l: (h, l, c, z))
    copies = jnp.broadcast_to(mine, (8, *mine.shape))
    row = lax.all_to_all(copies, "dist", split_axis=0, concat_axis=0, tiled=True)
    row = row.reshape(GRID, GRID * GRID)
    pieces = []
    for k in ORDER:
        piece = turned
        if k:
            piece = moved(turned, lambda h, z, c, l, k=k: (h, (z + k) % 8, c, l))
        pieces.append(piece)
    col = jnp.stack(pieces)
    far = []
    for i in range(2):
        half = jnp.stack(pieces[4 * i : 4 * i + 4])
        far.append(moved(half, lambda h, z, c, l: (1 - h, z, c, l)))
    core_col = moved(col, lambda h, z, c, l: (h, z, 1 - c, l))
    place = ((lax.axis_index("grp") >> 1) & 7).astype(jnp.int32).reshape(1)
    left, right = tables()
    green = green_table()
    partial = solve(place, row, col, core_col, left, right, green)
    far, partial = lax.optimization_barrier((far, partial))
    far_col = jnp.concatenate(far)
    far_core_col = moved(far_col, lambda h, z, c, l: (h, z, 1 - c, l))
    partial = solve(place, row, far_col, far_core_col, left, right, green, partial)
    sent = partial.astype(jnp.float16).reshape(8, 8, GRID * GRID + 128)
    arrived = lax.all_to_all(sent, "dist", split_axis=0, concat_axis=0, tiled=True)
    power = lax.optimization_barrier(arrived[:, 0:1, GRID * GRID : GRID * GRID + 1])
    terms = arrived[:, :, : GRID * GRID].astype(jnp.float32) * jnp.exp2(power.astype(jnp.float32))
    return terms.sum(axis=0)[None]


def solution(mesh):
    in_specs = (P("grp", "dist", None), P("grp"))
    out_specs = P("grp", "dist", None)
    return jax.shard_map(body, mesh=mesh, in_specs=in_specs, out_specs=out_specs, check_vma=False)
```

```python
import functools
import math

import jax
import jax.numpy as jnp
import numpy as np
from jax import lax
from jax.experimental import pallas as pl
from jax.experimental.pallas import tpu as pltpu
from jax.sharding import PartitionSpec as P

GRID = 64
GM = 32
PITCH = 65
box_length = 7.0


def split(x):
    hi = x.astype(jnp.bfloat16)
    lo = (x - hi.astype(jnp.float32)).astype(jnp.bfloat16)
    return hi, lo


def tables():
    position = np.arange(GRID)
    angles = (position[:, None] * position[None, :] % GRID) * (2.0 * math.pi / GRID)
    t = np.cos(angles) + np.sin(angles)
    hi = t.astype(jnp.bfloat16)
    lo = (t - hi.astype(np.float64)).astype(jnp.bfloat16)
    hi, lo = jnp.asarray(hi), jnp.asarray(lo)
    left = jnp.concatenate([hi, hi, lo], axis=1)
    zero = jnp.zeros_like(hi)
    two = lambda m: jnp.concatenate([jnp.concatenate([m, zero], 1), jnp.concatenate([zero, m], 1)], 0)
    wide = jnp.concatenate([two(hi), two(lo)], axis=1)
    right = jnp.concatenate([wide, wide], axis=0)
    return left, right


def green_table():
    p = jnp.arange(GRID, dtype=jnp.int32)
    f = jnp.minimum(p, GRID - p)
    sq = (f * f).astype(jnp.float32)
    tot = sq[:, None, None] + sq[None, :, None] + jnp.concatenate([sq, sq])[None, None, :]
    c = box_length**2 / (math.pi * GRID**3)
    return jnp.where(tot > 0.5, c / jnp.maximum(tot, 1.0), 0.0)


def dot(a, b):
    return jnp.dot(a, b, preferred_element_type=jnp.float32)


def along_lanes(x, right):
    hi, lo = split(x)
    y = dot(jnp.concatenate([hi, lo], axis=1), right)
    return y[:, :128] + y[:, 128:]


def along_rows(left, x):
    hi, lo = split(x)
    return dot(left, jnp.concatenate([hi, lo, hi], axis=0))


def solve_kernel(first, seat_ref, row_ref, *refs):
    sources = ((refs[0], refs[1]), (refs[2], refs[3]))
    left_ref, right_ref, green_ref = refs[4:7]
    col_ref, f_ref = refs[-2:]
    out_ref = refs[-3]
    group = seat_ref[0]
    core = jnp.bitwise_and(group, 1)
    z = jnp.bitwise_and(jnp.right_shift(group, 1), 7)

    for member in range(2):
        for block in range(8):
            away = jnp.bitwise_and(block - z + 8, 7)
            hops = jnp.where(away > 4, 8 - away, away)
            single = jnp.logical_or(away == 0, away == 4)
            holder = jnp.where(single, member, jnp.where(away > 4, 0, 1))
            paired = 8 - 2 * hops + jnp.bitwise_xor(holder, member)
            index = jnp.where(single, jnp.right_shift(away, 2), paired)
            rows = slice(8 * block, 8 * block + 8)
            for other in range(2):
                for half in range(2):
                    here = jnp.bitwise_xor(holder, core) == other
                    here = jnp.logical_and(here, jnp.right_shift(index, 2) == half)

                    @pl.when(here)
                    def _():
                        piece = sources[other][half][jnp.bitwise_and(index, 3)]
                        col_ref[member, rows, :] = piece.astype(jnp.float32)

    left = left_ref[...]
    right = right_ref[...]
    low = lax.broadcasted_iota(jnp.int32, (GRID, 128), 1) < 64

    packed = []
    for i in range(32):
        lanes = slice(128 * i, 128 * i + 128)
        row = row_ref[:, lanes].astype(jnp.float32)
        d1 = row * col_ref[0, :, lanes]
        d2 = row * col_ref[1, :, lanes]
        packed.append(jnp.where(low, d1, pltpu.roll(d2, 64, 1)))
        packed.append(jnp.where(low, pltpu.roll(d1, 64, 1), d2))
    g = along_lanes(jnp.concatenate(packed, axis=0), right)
    wide = jnp.concatenate([g[64 * i : 64 * i + 64] for i in range(64)], axis=1)
    h = along_rows(left, wide)
    for i in range(64):
        f_ref[PITCH * i : PITCH * i + 64, :] = h[:, 128 * i : 128 * i + 128]

    def middle(step, _):
        kx = step * GM
        parts = [f_ref[pl.ds(kx + i, 64, stride=PITCH), :] for i in range(GM)]
        h = along_rows(left, jnp.concatenate(parts, axis=1))
        h = h * jnp.concatenate([green_ref[kx + i] for i in range(GM)], axis=1)
        u = along_rows(left, h)
        for i in range(GM):
            f_ref[pl.ds(kx + i, 64, stride=PITCH), :] = u[:, 128 * i : 128 * i + 128]
        return 0

    lax.fori_loop(0, 64 // GM, middle, 0)

    occ = [-col_ref[member, 0:1, 4096:4224] for member in range(2)]
    wide = jnp.concatenate([f_ref[PITCH * i : PITCH * i + 64, :] for i in range(64)], axis=1)
    g = along_rows(left, wide)
    tall = jnp.concatenate([g[:, 128 * i : 128 * i + 128] for i in range(64)], axis=0)
    p = along_lanes(tall, right)
    for i in range(32):
        lanes = slice(128 * i, 128 * i + 128)
        p0, p1 = p[128 * i : 128 * i + 64], p[128 * i + 64 : 128 * i + 128]
        v1 = jnp.where(low, p0, pltpu.roll(p1, 64, 1))
        v2 = jnp.where(low, pltpu.roll(p0, 64, 1), p1)
        term = v1 * (col_ref[0, :, lanes] * occ[0]) + v2 * (col_ref[1, :, lanes] * occ[1])
        if not first:
            term = refs[7][:, lanes] + term
        out_ref[:, lanes] = term

    if not first:
        level = jnp.zeros((GRID, 128), jnp.float32)
        for i in range(32):
            level = jnp.maximum(level, jnp.abs(out_ref[:, 128 * i : 128 * i + 128]))
        peak = jnp.maximum(jnp.max(level, axis=(0, 1), keepdims=True), 1e-30)
        power = jnp.ceil(jnp.log2(jnp.broadcast_to(peak, (8, 128)))) - 15.0
        factor = jnp.exp2(-power)[0:1]
        for i in range(32):
            lanes = slice(128 * i, 128 * i + 128)
            out_ref[:, lanes] = out_ref[:, lanes] * factor
        out_ref[:, 4096:4224] = jnp.broadcast_to(power[0:1], (GRID, 128))


def solve(seat, row, mine, other, left, right, green, *more):
    vm = pl.BlockSpec(memory_space=pltpu.VMEM)
    sm = pl.BlockSpec(memory_space=pltpu.SMEM)
    width = GRID * GRID + (128 if more else 0)
    return pl.pallas_call(
        functools.partial(solve_kernel, not more),
        out_shape=jax.ShapeDtypeStruct((GRID, width), jnp.float32),
        in_specs=[sm] + [vm] * (8 + len(more)),
        out_specs=vm,
        scratch_shapes=[
            pltpu.VMEM((2, GRID, GRID * GRID + 128), jnp.float32),
            pltpu.VMEM((GRID * PITCH, 128), jnp.float32),
        ],
        cost_estimate=pl.CostEstimate(flops=10**10, bytes_accessed=10**7, transcendentals=0),
        compiler_params=pltpu.CompilerParams(vmem_limit_bytes=40 * 2**20),
        name="solve",
    )(seat, row, *mine, *other, left, right, green, *more)


AXES = ("grp", "dist")


def device(half, z, core, lane):
    return ((half * 8 + z) * 2 + core) * 8 + lane


def moved(x, rule):
    pairs = [
        (device(h, z, c, l), device(*rule(h, z, c, l)))
        for h in range(2)
        for z in range(8)
        for c in range(2)
        for l in range(8)
    ]
    return lax.ppermute(x, AXES, pairs)


def body(orbitals, occupations):
    return exchange(orbitals[0], occupations[0])


def cores(h, z, c, l):
    return (h, z, 1 - c, l)


def exchange(mine, occupation):
    slice_out = jnp.concatenate([mine, jnp.broadcast_to(occupation, (8, 128))], axis=1)
    kept = moved(slice_out, lambda h, z, c, l: (h, l, c, z))
    crossed = moved(slice_out, lambda h, z, c, l: (h, l, 1 - c, z))
    copies = jnp.broadcast_to(mine, (8, *mine.shape))
    row = lax.all_to_all(copies, "dist", split_axis=0, concat_axis=0, tiled=True)
    row = row.reshape(GRID, GRID * GRID)
    pair = jnp.stack([kept, crossed])
    fourth = moved(kept, lambda h, z, c, l: (h, (z + 4) % 8, c, l))
    shifted = {}
    for k in (3, 2, 1):
        rule = lambda h, z, c, l, k=k: (h, (z + (k if c == 0 else 8 - k)) % 8, c, l)
        shifted[k] = moved(pair, rule)
    halves = [
        jnp.concatenate([kept[None], fourth[None], shifted[3]]),
        jnp.concatenate([shifted[2], shifted[1]]),
    ]
    far, core = [], []
    for half in halves:
        far.append(moved(half, lambda h, z, c, l: (1 - h, z, c, l)))
        core.append(moved(half, cores))
    far_core = [moved(far[0], cores)]
    seat = lax.axis_index("grp").astype(jnp.int32).reshape(1)
    left, right = tables()
    green = green_table()
    partial = solve(seat, row, halves, core, left, right, green)
    last, partial = lax.optimization_barrier((far[1], partial))
    far[1] = last
    far_core.append(moved(last, cores))
    partial = solve(seat, row, far, far_core, left, right, green, partial)
    sent = partial.astype(jnp.float16).reshape(8, 8, GRID * GRID + 128)
    arrived = lax.all_to_all(sent, "dist", split_axis=0, concat_axis=0, tiled=True)
    power = lax.optimization_barrier(arrived[:, 0:1, GRID * GRID : GRID * GRID + 1])
    terms = arrived[:, :, : GRID * GRID].astype(jnp.float32) * jnp.exp2(power.astype(jnp.float32))
    return terms.sum(axis=0)[None]


def solution(mesh):
    in_specs = (P("grp", "dist", None), P("grp"))
    out_specs = P("grp", "dist", None)
    return jax.shard_map(body, mesh=mesh, in_specs=in_specs, out_specs=out_specs, check_vma=False)
```

```python
import functools
import math

import jax
import jax.numpy as jnp
import numpy as np
from jax import lax
from jax.experimental import pallas as pl
from jax.experimental.pallas import tpu as pltpu
from jax.sharding import PartitionSpec as P

GRID = 64
GM = 32
PITCH = 65
box_length = 7.0


def split(x):
    hi = x.astype(jnp.bfloat16)
    lo = (x - hi.astype(jnp.float32)).astype(jnp.bfloat16)
    return hi, lo


def tables():
    position = np.arange(GRID)
    angles = (position[:, None] * position[None, :] % GRID) * (2.0 * math.pi / GRID)
    t = np.cos(angles) + np.sin(angles)
    hi = t.astype(jnp.bfloat16)
    lo = (t - hi.astype(np.float64)).astype(jnp.bfloat16)
    hi, lo = jnp.asarray(hi), jnp.asarray(lo)
    left = jnp.concatenate([hi, hi, lo], axis=1)
    zero = jnp.zeros_like(hi)
    two = lambda m: jnp.concatenate([jnp.concatenate([m, zero], 1), jnp.concatenate([zero, m], 1)], 0)
    wide = jnp.concatenate([two(hi), two(lo)], axis=1)
    right = jnp.concatenate([wide, wide], axis=0)
    return left, right


def green_table():
    p = jnp.arange(GRID, dtype=jnp.int32)
    f = jnp.minimum(p, GRID - p)
    sq = (f * f).astype(jnp.float32)
    tot = sq[:, None, None] + sq[None, :, None] + jnp.concatenate([sq, sq])[None, None, :]
    c = box_length**2 / (math.pi * GRID**3)
    return jnp.where(tot > 0.5, c / jnp.maximum(tot, 1.0), 0.0)


def dot(a, b):
    return jnp.dot(a, b, preferred_element_type=jnp.float32)


def along_lanes(x, right):
    hi, lo = split(x)
    y = dot(jnp.concatenate([hi, lo], axis=1), right)
    return y[:, :128] + y[:, 128:]


def along_rows(left, x):
    hi, lo = split(x)
    return dot(left, jnp.concatenate([hi, lo, hi], axis=0))


def solve_kernel(first, seat_ref, row_ref, *refs):
    sources = ((refs[0], refs[1]), (refs[2], refs[3]))
    left_ref, right_ref, green_ref = refs[4:7]
    col_ref, f_ref = refs[-2:]
    out_ref = refs[-3]
    group = seat_ref[0]
    core = jnp.bitwise_and(group, 1)
    z = jnp.bitwise_and(jnp.right_shift(group, 1), 7)

    for member in range(2):
        for block in range(8):
            away = jnp.bitwise_and(block - z + 8, 7)
            hops = jnp.where(away > 4, 8 - away, away)
            single = jnp.logical_or(away == 0, away == 4)
            holder = jnp.where(single, member, jnp.where(away > 4, 0, 1))
            paired = jnp.where(hops == 1, 6, 6 - 2 * hops) + jnp.bitwise_xor(holder, member)
            index = jnp.where(single, 4 + jnp.right_shift(away, 2), paired)
            rows = slice(8 * block, 8 * block + 8)
            for other in range(2):
                for half in range(2):
                    here = jnp.bitwise_xor(holder, core) == other
                    here = jnp.logical_and(here, jnp.right_shift(index, 2) == half)

                    @pl.when(here)
                    def _():
                        piece = sources[other][half][jnp.bitwise_and(index, 3)]
                        col_ref[member, rows, :] = piece.astype(jnp.float32)

    left = left_ref[...]
    right = right_ref[...]
    low = lax.broadcasted_iota(jnp.int32, (GRID, 128), 1) < 64

    packed = []
    for i in range(32):
        lanes = slice(128 * i, 128 * i + 128)
        row = row_ref[:, lanes].astype(jnp.float32)
        d1 = row * col_ref[0, :, lanes]
        d2 = row * col_ref[1, :, lanes]
        packed.append(jnp.where(low, d1, pltpu.roll(d2, 64, 1)))
        packed.append(jnp.where(low, pltpu.roll(d1, 64, 1), d2))
    g = along_lanes(jnp.concatenate(packed, axis=0), right)
    wide = jnp.concatenate([g[64 * i : 64 * i + 64] for i in range(64)], axis=1)
    h = along_rows(left, wide)
    for i in range(64):
        f_ref[PITCH * i : PITCH * i + 64, :] = h[:, 128 * i : 128 * i + 128]

    def middle(step, _):
        kx = step * GM
        parts = [f_ref[pl.ds(kx + i, 64, stride=PITCH), :] for i in range(GM)]
        h = along_rows(left, jnp.concatenate(parts, axis=1))
        h = h * jnp.concatenate([green_ref[kx + i] for i in range(GM)], axis=1)
        u = along_rows(left, h)
        for i in range(GM):
            f_ref[pl.ds(kx + i, 64, stride=PITCH), :] = u[:, 128 * i : 128 * i + 128]
        return 0

    lax.fori_loop(0, 64 // GM, middle, 0)

    occ = [-col_ref[member, 0:1, 4096:4224] for member in range(2)]
    wide = jnp.concatenate([f_ref[PITCH * i : PITCH * i + 64, :] for i in range(64)], axis=1)
    g = along_rows(left, wide)
    tall = jnp.concatenate([g[:, 128 * i : 128 * i + 128] for i in range(64)], axis=0)
    p = along_lanes(tall, right)
    for i in range(32):
        lanes = slice(128 * i, 128 * i + 128)
        p0, p1 = p[128 * i : 128 * i + 64], p[128 * i + 64 : 128 * i + 128]
        v1 = jnp.where(low, p0, pltpu.roll(p1, 64, 1))
        v2 = jnp.where(low, pltpu.roll(p0, 64, 1), p1)
        term = v1 * (col_ref[0, :, lanes] * occ[0]) + v2 * (col_ref[1, :, lanes] * occ[1])
        if not first:
            term = refs[7][:, lanes] + term
        out_ref[:, lanes] = term

    if not first:
        level = jnp.zeros((GRID, 128), jnp.float32)
        for i in range(32):
            level = jnp.maximum(level, jnp.abs(out_ref[:, 128 * i : 128 * i + 128]))
        peak = jnp.maximum(jnp.max(level, axis=(0, 1), keepdims=True), 1e-30)
        power = jnp.ceil(jnp.log2(jnp.broadcast_to(peak, (8, 128)))) - 15.0
        factor = jnp.exp2(-power)[0:1]
        for i in range(32):
            lanes = slice(128 * i, 128 * i + 128)
            out_ref[:, lanes] = out_ref[:, lanes] * factor
        out_ref[:, 4096:4224] = jnp.broadcast_to(power[0:1], (GRID, 128))


def solve(seat, row, mine, other, left, right, green, *more):
    vm = pl.BlockSpec(memory_space=pltpu.VMEM)
    sm = pl.BlockSpec(memory_space=pltpu.SMEM)
    width = GRID * GRID + (128 if more else 0)
    return pl.pallas_call(
        functools.partial(solve_kernel, not more),
        out_shape=jax.ShapeDtypeStruct((GRID, width), jnp.float32),
        in_specs=[sm] + [vm] * (8 + len(more)),
        out_specs=vm,
        scratch_shapes=[
            pltpu.VMEM((2, GRID, GRID * GRID + 128), jnp.float32),
            pltpu.VMEM((GRID * PITCH, 128), jnp.float32),
        ],
        cost_estimate=pl.CostEstimate(flops=10**10, bytes_accessed=10**7, transcendentals=0),
        compiler_params=pltpu.CompilerParams(vmem_limit_bytes=40 * 2**20),
        name="solve",
    )(seat, row, *mine, *other, left, right, green, *more)


AXES = ("grp", "dist")


def device(half, z, core, lane):
    return ((half * 8 + z) * 2 + core) * 8 + lane


def moved(x, rule):
    pairs = [
        (device(h, z, c, l), device(*rule(h, z, c, l)))
        for h in range(2)
        for z in range(8)
        for c in range(2)
        for l in range(8)
    ]
    return lax.ppermute(x, AXES, pairs)


def body(orbitals, occupations):
    return exchange(orbitals[0], occupations[0])


def cores(h, z, c, l):
    return (h, z, 1 - c, l)


def ring(k):
    return lambda h, z, c, l: (h, (z + (k if c == 0 else 8 - k)) % 8, c, l)


def exchange(mine, occupation):
    slice_out = jnp.concatenate([mine, jnp.broadcast_to(occupation, (8, 128))], axis=1)
    kept = moved(slice_out, lambda h, z, c, l: (h, l, c, z))
    copies = jnp.broadcast_to(mine, (8, *mine.shape))
    row = lax.all_to_all(copies, "dist", split_axis=0, concat_axis=0, tiled=True)
    row = row.reshape(GRID, GRID * GRID)
    seat = lax.axis_index("grp").astype(jnp.int32).reshape(1)
    left, right = (jnp.where(seat[0] >= 0, t, 0) for t in tables())
    left, right, green, kept = lax.optimization_barrier((left, right, green_table(), kept))
    crossed = moved(kept, cores)
    pair = jnp.stack([kept, crossed])
    shifted = {}
    for k in (3, 2, 1):
        shifted[k] = moved(pair, ring(k))
    fourth = moved(shifted[3][0], ring(1))
    halves = [
        jnp.concatenate([shifted[3], shifted[2]]),
        jnp.concatenate([kept[None], fourth[None], shifted[1]]),
    ]
    far, core = [], []
    for half in halves:
        far.append(moved(half, lambda h, z, c, l: (1 - h, z, c, l)))
        core.append(moved(half, cores))
    partial = solve(seat, row, halves, core, left, right, green)
    far, partial = lax.optimization_barrier((far, partial))
    far_core = []
    for half in far:
        far_core.append(moved(half, cores))
    partial = solve(seat, row, far, far_core, left, right, green, partial)
    sent = partial.astype(jnp.float16).reshape(8, 8, GRID * GRID + 128)
    arrived = lax.all_to_all(sent, "dist", split_axis=0, concat_axis=0, tiled=True)
    power = lax.optimization_barrier(arrived[:, 0:1, GRID * GRID : GRID * GRID + 1])
    terms = arrived[:, :, : GRID * GRID].astype(jnp.float32) * jnp.exp2(power.astype(jnp.float32))
    return terms.sum(axis=0)[None]


def solution(mesh):
    in_specs = (P("grp", "dist", None), P("grp"))
    out_specs = P("grp", "dist", None)
    return jax.shard_map(body, mesh=mesh, in_specs=in_specs, out_specs=out_specs, check_vma=False)
```

```python
import functools
import math

import jax
import jax.numpy as jnp
import numpy as np
from jax import lax
from jax.experimental import pallas as pl
from jax.experimental.pallas import tpu as pltpu
from jax.sharding import PartitionSpec as P

GRID = 64
GM = 32
PITCH = 65
box_length = 7.0


def split(x):
    hi = x.astype(jnp.bfloat16)
    lo = (x - hi.astype(jnp.float32)).astype(jnp.bfloat16)
    return hi, lo


def tables():
    position = np.arange(GRID)
    angles = (position[:, None] * position[None, :] % GRID) * (2.0 * math.pi / GRID)
    t = np.cos(angles) + np.sin(angles)
    hi = t.astype(jnp.bfloat16)
    lo = (t - hi.astype(np.float64)).astype(jnp.bfloat16)
    hi, lo = jnp.asarray(hi), jnp.asarray(lo)
    left = jnp.concatenate([hi, hi, lo], axis=1)
    zero = jnp.zeros_like(hi)
    two = lambda m: jnp.concatenate([jnp.concatenate([m, zero], 1), jnp.concatenate([zero, m], 1)], 0)
    wide = jnp.concatenate([two(hi), two(lo)], axis=1)
    right = jnp.concatenate([wide, wide], axis=0)
    return left, right


def green_table(live):
    p = jnp.arange(GRID, dtype=jnp.int32)
    f = jnp.minimum(p, GRID - p)
    sq = (f * f).astype(jnp.float32)
    tot = sq[:, None, None] + sq[None, :, None] + jnp.concatenate([sq, sq])[None, None, :]
    c = jnp.where(live, box_length**2 / (math.pi * GRID**3), 0.0)
    return jnp.where(tot > 0.5, c / jnp.maximum(tot, 1.0), 0.0)


def dot(a, b):
    return jnp.dot(a, b, preferred_element_type=jnp.float32)


def along_lanes(x, right):
    hi, lo = split(x)
    y = dot(jnp.concatenate([hi, lo], axis=1), right)
    return y[:, :128] + y[:, 128:]


def along_rows(left, x):
    hi, lo = split(x)
    return dot(left, jnp.concatenate([hi, lo, hi], axis=0))


def solve_kernel(first, seat_ref, row_ref, *refs):
    sources = ((refs[0], refs[1]), (refs[2], refs[3]))
    left_ref, right_ref, green_ref = refs[4:7]
    col_ref, f_ref = refs[-2:]
    out_ref = refs[-3]
    group = seat_ref[0]
    core = jnp.bitwise_and(group, 1)
    z = jnp.bitwise_and(jnp.right_shift(group, 1), 7)

    for member in range(2):
        for block in range(8):
            away = jnp.bitwise_and(block - z + 8, 7)
            hops = jnp.where(away > 4, 8 - away, away)
            single = jnp.logical_or(away == 0, away == 4)
            holder = jnp.where(single, member, jnp.where(away > 4, 0, 1))
            early = jnp.logical_or(away == 0, hops == 1)
            paired = jnp.where(hops == 2, 3, 1) + jnp.bitwise_xor(holder, member)
            index = jnp.where(single, 0, paired)
            rows = slice(8 * block, 8 * block + 8)
            for other in range(2):
                for half in range(2):
                    here = jnp.bitwise_xor(holder, core) == other
                    here = jnp.logical_and(here, early == (half == 0))

                    @pl.when(here)
                    def _():
                        piece = sources[other][half][index]
                        col_ref[member, rows, :] = piece.astype(jnp.float32)

    left = left_ref[...]
    right = right_ref[...]
    low = lax.broadcasted_iota(jnp.int32, (GRID, 128), 1) < 64

    packed = []
    for i in range(32):
        lanes = slice(128 * i, 128 * i + 128)
        row = row_ref[:, lanes].astype(jnp.float32)
        d1 = row * col_ref[0, :, lanes]
        d2 = row * col_ref[1, :, lanes]
        packed.append(jnp.where(low, d1, pltpu.roll(d2, 64, 1)))
        packed.append(jnp.where(low, pltpu.roll(d1, 64, 1), d2))
    g = along_lanes(jnp.concatenate(packed, axis=0), right)
    wide = jnp.concatenate([g[64 * i : 64 * i + 64] for i in range(64)], axis=1)
    h = along_rows(left, wide)
    for i in range(64):
        f_ref[PITCH * i : PITCH * i + 64, :] = h[:, 128 * i : 128 * i + 128]

    def middle(step, _):
        kx = step * GM
        parts = [f_ref[pl.ds(kx + i, 64, stride=PITCH), :] for i in range(GM)]
        h = along_rows(left, jnp.concatenate(parts, axis=1))
        h = h * jnp.concatenate([green_ref[kx + i] for i in range(GM)], axis=1)
        u = along_rows(left, h)
        for i in range(GM):
            f_ref[pl.ds(kx + i, 64, stride=PITCH), :] = u[:, 128 * i : 128 * i + 128]
        return 0

    lax.fori_loop(0, 64 // GM, middle, 0)

    occ = [-col_ref[member, 0:1, 4096:4224] for member in range(2)]
    wide = jnp.concatenate([f_ref[PITCH * i : PITCH * i + 64, :] for i in range(64)], axis=1)
    g = along_rows(left, wide)
    tall = jnp.concatenate([g[:, 128 * i : 128 * i + 128] for i in range(64)], axis=0)
    p = along_lanes(tall, right)
    for i in range(32):
        lanes = slice(128 * i, 128 * i + 128)
        p0, p1 = p[128 * i : 128 * i + 64], p[128 * i + 64 : 128 * i + 128]
        v1 = jnp.where(low, p0, pltpu.roll(p1, 64, 1))
        v2 = jnp.where(low, pltpu.roll(p0, 64, 1), p1)
        term = v1 * (col_ref[0, :, lanes] * occ[0]) + v2 * (col_ref[1, :, lanes] * occ[1])
        if not first:
            term = refs[7][:, lanes] + term
        out_ref[:, lanes] = term

    if not first:
        level = jnp.zeros((GRID, 128), jnp.float32)
        for i in range(32):
            level = jnp.maximum(level, jnp.abs(out_ref[:, 128 * i : 128 * i + 128]))
        peak = jnp.maximum(jnp.max(level, axis=(0, 1), keepdims=True), 1e-30)
        power = jnp.ceil(jnp.log2(jnp.broadcast_to(peak, (8, 128)))) - 15.0
        factor = jnp.exp2(-power)[0:1]
        for i in range(32):
            lanes = slice(128 * i, 128 * i + 128)
            out_ref[:, lanes] = out_ref[:, lanes] * factor
        out_ref[:, 4096:4224] = jnp.broadcast_to(power[0:1], (GRID, 128))


def solve(seat, row, mine, other, left, right, green, *more):
    vm = pl.BlockSpec(memory_space=pltpu.VMEM)
    sm = pl.BlockSpec(memory_space=pltpu.SMEM)
    width = GRID * GRID + (128 if more else 0)
    return pl.pallas_call(
        functools.partial(solve_kernel, not more),
        out_shape=jax.ShapeDtypeStruct((GRID, width), jnp.float32),
        in_specs=[sm] + [vm] * (8 + len(more)),
        out_specs=vm,
        scratch_shapes=[
            pltpu.VMEM((2, GRID, GRID * GRID + 128), jnp.float32),
            pltpu.VMEM((GRID * PITCH, 128), jnp.float32),
        ],
        cost_estimate=pl.CostEstimate(flops=10**10, bytes_accessed=10**7, transcendentals=0),
        compiler_params=pltpu.CompilerParams(vmem_limit_bytes=40 * 2**20),
        name="solve",
    )(seat, row, *mine, *other, left, right, green, *more)


AXES = ("grp", "dist")


def device(half, z, core, lane):
    return ((half * 8 + z) * 2 + core) * 8 + lane


def moved(x, rule):
    pairs = [
        (device(h, z, c, l), device(*rule(h, z, c, l)))
        for h in range(2)
        for z in range(8)
        for c in range(2)
        for l in range(8)
    ]
    return lax.ppermute(x, AXES, pairs)


def body(orbitals, occupations):
    return exchange(orbitals[0], occupations[0])


def cores(h, z, c, l):
    return (h, z, 1 - c, l)


def ring(k):
    return lambda h, z, c, l: (h, (z + (k if c == 0 else 8 - k)) % 8, c, l)


def exchange(mine, occupation):
    slice_out = jnp.concatenate([mine, jnp.broadcast_to(occupation, (8, 128))], axis=1)
    kept = moved(slice_out, lambda h, z, c, l: (h, l, c, z))
    copies = jnp.broadcast_to(mine, (8, *mine.shape))
    row = lax.all_to_all(copies, "dist", split_axis=0, concat_axis=0, tiled=True)
    row = row.reshape(GRID, GRID * GRID)
    crossed = moved(kept, cores)
    seat = lax.axis_index("grp").astype(jnp.int32).reshape(1)
    pair, seat = lax.optimization_barrier((jnp.stack([kept, crossed]), seat))
    live = seat[0] >= 0
    left, right = tables()
    left = jnp.where(live, left, 0)
    right = jnp.where(live, right, 0)
    green = green_table(live)
    shifted = {}
    for k in (1, 3, 2):
        shifted[k] = moved(pair, ring(k))
    third, left, right, green = lax.optimization_barrier((shifted[3], left, right, green))
    fourth = moved(third[0], ring(1))
    halves = [
        jnp.concatenate([kept[None], shifted[1]]),
        jnp.concatenate([fourth[None], third, shifted[2]]),
    ]
    far, core = [], []
    for half in halves:
        far.append(moved(half, lambda h, z, c, l: (1 - h, z, c, l)))
        core.append(moved(half, cores))
    far_core = [moved(far[0], cores)]
    partial = solve(seat, row, halves, core, left, right, green)
    far[1], partial = lax.optimization_barrier((far[1], partial))
    far_core.append(moved(far[1], cores))
    partial = solve(seat, row, far, far_core, left, right, green, partial)
    sent = partial.astype(jnp.float16).reshape(8, 8, GRID * GRID + 128)
    arrived = lax.all_to_all(sent, "dist", split_axis=0, concat_axis=0, tiled=True)
    power = lax.optimization_barrier(arrived[:, 0:1, GRID * GRID : GRID * GRID + 1])
    terms = arrived[:, :, : GRID * GRID].astype(jnp.float32) * jnp.exp2(power.astype(jnp.float32))
    return terms.sum(axis=0)[None]


def solution(mesh):
    in_specs = (P("grp", "dist", None), P("grp"))
    out_specs = P("grp", "dist", None)
    return jax.shard_map(body, mesh=mesh, in_specs=in_specs, out_specs=out_specs, check_vma=False)
```

```python
import functools
import math

import jax
import jax.numpy as jnp
import numpy as np
from jax import lax
from jax.experimental import pallas as pl
from jax.experimental.pallas import tpu as pltpu
from jax.sharding import PartitionSpec as P

GRID = 64
GM = 32
PITCH = 65
box_length = 7.0


def split(x):
    hi = x.astype(jnp.bfloat16)
    lo = (x - hi.astype(jnp.float32)).astype(jnp.bfloat16)
    return hi, lo


def tables():
    position = np.arange(GRID)
    angles = (position[:, None] * position[None, :] % GRID) * (2.0 * math.pi / GRID)
    t = np.cos(angles) + np.sin(angles)
    hi = t.astype(jnp.bfloat16)
    lo = (t - hi.astype(np.float64)).astype(jnp.bfloat16)
    hi, lo = jnp.asarray(hi), jnp.asarray(lo)
    left = jnp.concatenate([hi, hi, lo], axis=1)
    zero = jnp.zeros_like(hi)
    two = lambda m: jnp.concatenate([jnp.concatenate([m, zero], 1), jnp.concatenate([zero, m], 1)], 0)
    wide = jnp.concatenate([two(hi), two(lo)], axis=1)
    right = jnp.concatenate([wide, wide], axis=0)
    return left, right


def green_table(live):
    p = jnp.arange(GRID, dtype=jnp.int32)
    f = jnp.minimum(p, GRID - p)
    sq = (f * f).astype(jnp.float32)
    tot = sq[:, None, None] + sq[None, :, None] + jnp.concatenate([sq, sq])[None, None, :]
    c = jnp.where(live, box_length**2 / (math.pi * GRID**3), 0.0)
    return jnp.where(tot > 0.5, c / jnp.maximum(tot, 1.0), 0.0)


def dot(a, b):
    return jnp.dot(a, b, preferred_element_type=jnp.float32)


def along_lanes(x, right):
    hi, lo = split(x)
    y = dot(jnp.concatenate([hi, lo], axis=1), right)
    return y[:, :128] + y[:, 128:]


def along_rows(left, x):
    hi, lo = split(x)
    return dot(left, jnp.concatenate([hi, lo, hi], axis=0))


def solve_kernel(first, seat_ref, row_ref, *refs):
    pair_ref, near_refs, fourth_ref, other_refs = refs[0], refs[1:4], refs[4], refs[5:8]
    left_ref, right_ref, green_ref = refs[8:11]
    col_ref, f_ref = refs[-2:]
    out_ref = refs[-3]
    group = seat_ref[0]
    core = jnp.bitwise_and(group, 1)
    z = jnp.bitwise_and(jnp.right_shift(group, 1), 7)

    def place(ref, holder, block):
        rows = pl.ds(pl.multiple_of(8 * jnp.bitwise_and(block + 8, 7), 8), 8)
        for i in range(2):
            col_ref[jnp.bitwise_xor(i, holder), rows, :] = ref[i].astype(jnp.float32)

    place(pair_ref, core, z)
    place(fourth_ref, core, z + 4)
    for k in (1, 2, 3):
        step = jnp.where(core == 0, -k, k)
        place(near_refs[k - 1], core, z + step)
        place(other_refs[k - 1], 1 - core, z - step)

    left = left_ref[...]
    right = right_ref[...]
    low = lax.broadcasted_iota(jnp.int32, (GRID, 128), 1) < 64

    packed = []
    for i in range(32):
        lanes = slice(128 * i, 128 * i + 128)
        row = row_ref[:, lanes].astype(jnp.float32)
        d1 = row * col_ref[0, :, lanes]
        d2 = row * col_ref[1, :, lanes]
        packed.append(jnp.where(low, d1, pltpu.roll(d2, 64, 1)))
        packed.append(jnp.where(low, pltpu.roll(d1, 64, 1), d2))
    g = along_lanes(jnp.concatenate(packed, axis=0), right)
    wide = jnp.concatenate([g[64 * i : 64 * i + 64] for i in range(64)], axis=1)
    h = along_rows(left, wide)
    for i in range(64):
        f_ref[PITCH * i : PITCH * i + 64, :] = h[:, 128 * i : 128 * i + 128]

    def middle(step, _):
        kx = step * GM
        parts = [f_ref[pl.ds(kx + i, 64, stride=PITCH), :] for i in range(GM)]
        h = along_rows(left, jnp.concatenate(parts, axis=1))
        h = h * jnp.concatenate([green_ref[kx + i] for i in range(GM)], axis=1)
        u = along_rows(left, h)
        for i in range(GM):
            f_ref[pl.ds(kx + i, 64, stride=PITCH), :] = u[:, 128 * i : 128 * i + 128]
        return 0

    lax.fori_loop(0, 64 // GM, middle, 0)

    occ = [-col_ref[member, 0:1, 4096:4224] for member in range(2)]
    wide = jnp.concatenate([f_ref[PITCH * i : PITCH * i + 64, :] for i in range(64)], axis=1)
    g = along_rows(left, wide)
    tall = jnp.concatenate([g[:, 128 * i : 128 * i + 128] for i in range(64)], axis=0)
    p = along_lanes(tall, right)
    for i in range(32):
        lanes = slice(128 * i, 128 * i + 128)
        p0, p1 = p[128 * i : 128 * i + 64], p[128 * i + 64 : 128 * i + 128]
        v1 = jnp.where(low, p0, pltpu.roll(p1, 64, 1))
        v2 = jnp.where(low, pltpu.roll(p0, 64, 1), p1)
        term = v1 * (col_ref[0, :, lanes] * occ[0]) + v2 * (col_ref[1, :, lanes] * occ[1])
        if not first:
            term = refs[11][:, lanes] + term
        out_ref[:, lanes] = term

    if not first:
        level = jnp.zeros((GRID, 128), jnp.float32)
        for i in range(32):
            level = jnp.maximum(level, jnp.abs(out_ref[:, 128 * i : 128 * i + 128]))
        peak = jnp.maximum(jnp.max(level, axis=(0, 1), keepdims=True), 1e-30)
        power = jnp.ceil(jnp.log2(jnp.broadcast_to(peak, (8, 128)))) - 15.0
        factor = jnp.exp2(-power)[0:1]
        for i in range(32):
            lanes = slice(128 * i, 128 * i + 128)
            out_ref[:, lanes] = out_ref[:, lanes] * factor
        out_ref[:, 4096:4224] = jnp.broadcast_to(power[0:1], (GRID, 128))


def solve(seat, row, mine, other, left, right, green, *more):
    vm = pl.BlockSpec(memory_space=pltpu.VMEM)
    sm = pl.BlockSpec(memory_space=pltpu.SMEM)
    width = GRID * GRID + (128 if more else 0)
    return pl.pallas_call(
        functools.partial(solve_kernel, not more),
        out_shape=jax.ShapeDtypeStruct((GRID, width), jnp.float32),
        in_specs=[sm] + [vm] * (12 + len(more)),
        out_specs=vm,
        scratch_shapes=[
            pltpu.VMEM((2, GRID, GRID * GRID + 128), jnp.float32),
            pltpu.VMEM((GRID * PITCH, 128), jnp.float32),
        ],
        cost_estimate=pl.CostEstimate(flops=10**10, bytes_accessed=10**7, transcendentals=0),
        compiler_params=pltpu.CompilerParams(vmem_limit_bytes=32 * 2**20),
        name="solve",
    )(seat, row, *mine, *other, left, right, green, *more)


AXES = ("grp", "dist")


def device(half, z, core, lane):
    return ((half * 8 + z) * 2 + core) * 8 + lane


def moved(x, rule):
    pairs = [
        (device(h, z, c, l), device(*rule(h, z, c, l)))
        for h in range(2)
        for z in range(8)
        for c in range(2)
        for l in range(8)
    ]
    return lax.ppermute(x, AXES, pairs)


def body(orbitals, occupations):
    return exchange(orbitals[0], occupations[0])


def cores(h, z, c, l):
    return (h, z, 1 - c, l)


def halves(h, z, c, l):
    return (1 - h, z, c, l)


def ring(k):
    return lambda h, z, c, l: (h, (z + (k if c == 0 else 8 - k)) % 8, c, l)


def exchange(mine, occupation):
    slice_out = jnp.concatenate([mine, jnp.broadcast_to(occupation, (8, 128))], axis=1)
    kept = moved(slice_out, lambda h, z, c, l: (h, l, c, z))
    copies = jnp.broadcast_to(mine, (8, *mine.shape))
    row = lax.all_to_all(copies, "dist", split_axis=0, concat_axis=0, tiled=True)
    row = row.reshape(GRID, GRID * GRID)
    crossed = moved(kept, cores)
    seat = lax.axis_index("grp").astype(jnp.int32).reshape(1)
    pair, seat = lax.optimization_barrier((jnp.stack([kept, crossed]), seat))
    live = seat[0] >= 0
    left, right = tables()
    left = jnp.where(live, left, 0)
    right = jnp.where(live, right, 0)
    green = green_table(live)
    chain, far, core = [pair], [], [None]
    for k in range(5):
        if k == 2:
            chain[k], left, right, green = lax.optimization_barrier((chain[k], left, right, green))
        if k < 4:
            chain.append(moved(chain[k], ring(1)))
        if k in (1, 2, 3):
            core.append(moved(chain[k], cores))
        far.append(moved(chain[k], halves))
    far_core = []
    for k in (1, 2):
        far_core.append(moved(far[k], cores))
    partial = solve(seat, row, chain, core[1:], left, right, green)
    far[3], partial = lax.optimization_barrier((far[3], partial))
    far_core.append(moved(far[3], cores))
    partial = solve(seat, row, far, far_core, left, right, green, partial)
    sent = partial.astype(jnp.float16).reshape(8, 8, GRID * GRID + 128)
    arrived = lax.all_to_all(sent, "dist", split_axis=0, concat_axis=0, tiled=True)
    power = lax.optimization_barrier(arrived[:, 0:1, GRID * GRID : GRID * GRID + 1])
    terms = arrived[:, :, : GRID * GRID].astype(jnp.float32) * jnp.exp2(power.astype(jnp.float32))
    return terms.sum(axis=0)[None]


def solution(mesh):
    in_specs = (P("grp", "dist", None), P("grp"))
    out_specs = P("grp", "dist", None)
    return jax.shard_map(body, mesh=mesh, in_specs=in_specs, out_specs=out_specs, check_vma=False)
```

```python
import functools
import math

import jax
import jax.numpy as jnp
import numpy as np
from jax import lax
from jax.experimental import pallas as pl
from jax.experimental.pallas import tpu as pltpu
from jax.sharding import PartitionSpec as P

GRID = 64
GM = 32
PITCH = 65
box_length = 7.0


def split(x):
    hi = x.astype(jnp.bfloat16)
    lo = (x - hi.astype(jnp.float32)).astype(jnp.bfloat16)
    return hi, lo


def tables():
    position = np.arange(GRID)
    angles = (position[:, None] * position[None, :] % GRID) * (2.0 * math.pi / GRID)
    t = np.cos(angles) + np.sin(angles)
    hi = t.astype(jnp.bfloat16)
    lo = (t - hi.astype(np.float64)).astype(jnp.bfloat16)
    hi, lo = jnp.asarray(hi), jnp.asarray(lo)
    left = jnp.concatenate([hi, hi, lo], axis=1)
    zero = jnp.zeros_like(hi)
    two = lambda m: jnp.concatenate([jnp.concatenate([m, zero], 1), jnp.concatenate([zero, m], 1)], 0)
    wide = jnp.concatenate([two(hi), two(lo)], axis=1)
    right = jnp.concatenate([wide, wide], axis=0)
    return left, right


def green_table(live):
    p = jnp.arange(GRID, dtype=jnp.int32)
    f = jnp.minimum(p, GRID - p)
    sq = (f * f).astype(jnp.float32)
    tot = sq[:, None, None] + sq[None, :, None] + jnp.concatenate([sq, sq])[None, None, :]
    c = jnp.where(live, box_length**2 / (math.pi * GRID**3), 0.0)
    return jnp.where(tot > 0.5, c / jnp.maximum(tot, 1.0), 0.0)


def dot(a, b):
    return jnp.dot(a, b, preferred_element_type=jnp.float32)


def along_lanes(x, right):
    hi, lo = split(x)
    y = dot(jnp.concatenate([hi, lo], axis=1), right)
    return y[:, :128] + y[:, 128:]


def along_rows(left, x):
    hi, lo = split(x)
    return dot(left, jnp.concatenate([hi, lo, hi], axis=0))


def solve_kernel(first, seat_ref, row_ref, *refs):
    early_ref, late_ref, fourth_ref, other_early_ref, other_late_ref = refs[:5]
    left_ref, right_ref, green_ref = refs[5:8]
    col_ref, f_ref = refs[-2:]
    out_ref = refs[-3]
    group = seat_ref[0]
    core = jnp.bitwise_and(group, 1)
    z = jnp.bitwise_and(jnp.right_shift(group, 1), 7)

    def place(ref, start, holder, block):
        rows = pl.ds(pl.multiple_of(8 * jnp.bitwise_and(block + 8, 7), 8), 8)
        for i in range(2):
            col_ref[jnp.bitwise_xor(i, holder), rows, :] = ref[start + i].astype(jnp.float32)

    place(early_ref, 0, core, z)
    place(fourth_ref, 0, core, z + 4)
    sides = ((core, early_ref, late_ref), (1 - core, other_early_ref, other_late_ref))
    for holder, early, late in sides:
        sign = jnp.where(holder == 0, -1, 1)
        place(early, 2, holder, z + sign)
        place(late, 0, holder, z + 3 * sign)
        place(late, 2, holder, z + 2 * sign)

    left = left_ref[...]
    right = right_ref[...]
    low = lax.broadcasted_iota(jnp.int32, (GRID, 128), 1) < 64

    packed = []
    for i in range(32):
        lanes = slice(128 * i, 128 * i + 128)
        row = row_ref[:, lanes].astype(jnp.float32)
        d1 = row * col_ref[0, :, lanes]
        d2 = row * col_ref[1, :, lanes]
        packed.append(jnp.where(low, d1, pltpu.roll(d2, 64, 1)))
        packed.append(jnp.where(low, pltpu.roll(d1, 64, 1), d2))
    g = along_lanes(jnp.concatenate(packed, axis=0), right)
    wide = jnp.concatenate([g[64 * i : 64 * i + 64] for i in range(64)], axis=1)
    h = along_rows(left, wide)
    for i in range(64):
        f_ref[PITCH * i : PITCH * i + 64, :] = h[:, 128 * i : 128 * i + 128]

    def middle(step, _):
        kx = step * GM
        parts = [f_ref[pl.ds(kx + i, 64, stride=PITCH), :] for i in range(GM)]
        h = along_rows(left, jnp.concatenate(parts, axis=1))
        h = h * jnp.concatenate([green_ref[kx + i] for i in range(GM)], axis=1)
        u = along_rows(left, h)
        for i in range(GM):
            f_ref[pl.ds(kx + i, 64, stride=PITCH), :] = u[:, 128 * i : 128 * i + 128]
        return 0

    lax.fori_loop(0, 64 // GM, middle, 0)

    occ = [-col_ref[member, 0:1, 4096:4224] for member in range(2)]
    wide = jnp.concatenate([f_ref[PITCH * i : PITCH * i + 64, :] for i in range(64)], axis=1)
    g = along_rows(left, wide)
    tall = jnp.concatenate([g[:, 128 * i : 128 * i + 128] for i in range(64)], axis=0)
    p = along_lanes(tall, right)
    for i in range(32):
        lanes = slice(128 * i, 128 * i + 128)
        p0, p1 = p[128 * i : 128 * i + 64], p[128 * i + 64 : 128 * i + 128]
        v1 = jnp.where(low, p0, pltpu.roll(p1, 64, 1))
        v2 = jnp.where(low, pltpu.roll(p0, 64, 1), p1)
        term = v1 * (col_ref[0, :, lanes] * occ[0]) + v2 * (col_ref[1, :, lanes] * occ[1])
        if not first:
            term = refs[8][:, lanes] + term
        out_ref[:, lanes] = term

    if not first:
        level = jnp.zeros((GRID, 128), jnp.float32)
        for i in range(32):
            level = jnp.maximum(level, jnp.abs(out_ref[:, 128 * i : 128 * i + 128]))
        peak = jnp.maximum(jnp.max(level, axis=(0, 1), keepdims=True), 1e-30)
        power = jnp.ceil(jnp.log2(jnp.broadcast_to(peak, (8, 128)))) - 15.0
        factor = jnp.exp2(-power)[0:1]
        for i in range(32):
            lanes = slice(128 * i, 128 * i + 128)
            out_ref[:, lanes] = out_ref[:, lanes] * factor
        out_ref[:, 4096:4224] = jnp.broadcast_to(power[0:1], (GRID, 128))


def copies_kernel(x_ref, out_ref, sem):
    sends = [pltpu.make_async_copy(x_ref, out_ref.at[i], sem.at[i]) for i in range(8)]
    for send in sends:
        send.start()
    for send in sends:
        send.wait()


def copies_of(x):
    return pl.pallas_call(
        copies_kernel,
        out_shape=jax.ShapeDtypeStruct((8, *x.shape), x.dtype),
        in_specs=[pl.BlockSpec(memory_space=pltpu.VMEM)],
        out_specs=pl.BlockSpec(memory_space=pl.ANY),
        scratch_shapes=[pltpu.SemaphoreType.DMA((8,))],
        compiler_params=pltpu.CompilerParams(vmem_limit_bytes=2**20),
        name="copies",
    )(x)


def solve(seat, row, mine, other, left, right, green, *more):
    vm = pl.BlockSpec(memory_space=pltpu.VMEM)
    sm = pl.BlockSpec(memory_space=pltpu.SMEM)
    width = GRID * GRID + (128 if more else 0)
    return pl.pallas_call(
        functools.partial(solve_kernel, not more),
        out_shape=jax.ShapeDtypeStruct((GRID, width), jnp.float32),
        in_specs=[sm] + [vm] * (9 + len(more)),
        out_specs=vm,
        scratch_shapes=[
            pltpu.VMEM((2, GRID, GRID * GRID + 128), jnp.float32),
            pltpu.VMEM((GRID * PITCH, 128), jnp.float32),
        ],
        cost_estimate=pl.CostEstimate(flops=10**10, bytes_accessed=10**7, transcendentals=0),
        compiler_params=pltpu.CompilerParams(vmem_limit_bytes=32 * 2**20),
        name="solve",
    )(seat, row, *mine, *other, left, right, green, *more)


AXES = ("grp", "dist")


def device(half, z, core, lane):
    return ((half * 8 + z) * 2 + core) * 8 + lane


def moved(x, rule):
    pairs = [
        (device(h, z, c, l), device(*rule(h, z, c, l)))
        for h in range(2)
        for z in range(8)
        for c in range(2)
        for l in range(8)
    ]
    return lax.ppermute(x, AXES, pairs)


def body(orbitals, occupations):
    return exchange(orbitals[0], occupations[0])


def cores(h, z, c, l):
    return (h, z, 1 - c, l)


def halves(h, z, c, l):
    return (1 - h, z, c, l)


def ring(k):
    return lambda h, z, c, l: (h, (z + (k if c == 0 else 8 - k)) % 8, c, l)


def exchange(mine, occupation):
    slice_out = jnp.concatenate([mine, jnp.broadcast_to(occupation, (8, 128))], axis=1)
    kept = moved(slice_out, lambda h, z, c, l: (h, l, c, z))
    copies = copies_of(mine)
    row = lax.all_to_all(copies, "dist", split_axis=0, concat_axis=0, tiled=True)
    row = row.reshape(GRID, GRID * GRID)
    crossed = moved(kept, cores)
    seat = lax.axis_index("grp").astype(jnp.int32).reshape(1)
    pair, seat = lax.optimization_barrier((jnp.stack([kept, crossed]), seat))
    live = seat[0] >= 0
    left, right = tables()
    left = jnp.where(live, left, 0)
    right = jnp.where(live, right, 0)
    green = green_table(live)
    hop = {}
    for k in (1, 3, 2):
        hop[k] = moved(pair, ring(k))
    early = jnp.concatenate([pair, hop[1]])
    far_early = moved(early, halves)
    core_early = moved(early, cores)
    hop[3], left, right, green = lax.optimization_barrier((hop[3], left, right, green))
    fourth = moved(hop[3], ring(1))
    late = jnp.concatenate([hop[3], hop[2]])
    core_late = moved(late, cores)
    far_late = moved(late, halves)
    far_fourth = moved(fourth, halves)
    far_core_early = moved(far_early, cores)
    mine, other = (early, late, fourth), (core_early, core_late)
    partial = solve(seat, row, mine, other, left, right, green)
    far_late, partial = lax.optimization_barrier((far_late, partial))
    far_core_late = moved(far_late, cores)
    mine, other = (far_early, far_late, far_fourth), (far_core_early, far_core_late)
    partial = solve(seat, row, mine, other, left, right, green, partial)
    sent = partial.astype(jnp.float16).reshape(8, 8, GRID * GRID + 128)
    arrived = lax.all_to_all(sent, "dist", split_axis=0, concat_axis=0, tiled=True)
    power = lax.optimization_barrier(arrived[:, 0:1, GRID * GRID : GRID * GRID + 1])
    terms = arrived[:, :, : GRID * GRID].astype(jnp.float32) * jnp.exp2(power.astype(jnp.float32))
    return terms.sum(axis=0)[None]


def solution(mesh):
    in_specs = (P("grp", "dist", None), P("grp"))
    out_specs = P("grp", "dist", None)
    return jax.shard_map(body, mesh=mesh, in_specs=in_specs, out_specs=out_specs, check_vma=False)
```

```python
import functools
import math

import jax
import jax.numpy as jnp
import numpy as np
from jax import lax
from jax.experimental import pallas as pl
from jax.experimental.pallas import tpu as pltpu
from jax.sharding import PartitionSpec as P

GRID = 64
GM = 32
PITCH = 65
box_length = 7.0


def split(x):
    hi = x.astype(jnp.bfloat16)
    lo = (x - hi.astype(jnp.float32)).astype(jnp.bfloat16)
    return hi, lo


def tables():
    position = np.arange(GRID)
    angles = (position[:, None] * position[None, :] % GRID) * (2.0 * math.pi / GRID)
    t = np.cos(angles) + np.sin(angles)
    hi = t.astype(jnp.bfloat16)
    lo = (t - hi.astype(np.float64)).astype(jnp.bfloat16)
    hi, lo = jnp.asarray(hi), jnp.asarray(lo)
    left = jnp.concatenate([hi, hi, lo], axis=1)
    zero = jnp.zeros_like(hi)
    two = lambda m: jnp.concatenate([jnp.concatenate([m, zero], 1), jnp.concatenate([zero, m], 1)], 0)
    wide = jnp.concatenate([two(hi), two(lo)], axis=1)
    right = jnp.concatenate([wide, wide], axis=0)
    return left, right


def green_table(live):
    p = jnp.arange(GRID, dtype=jnp.int32)
    f = jnp.minimum(p, GRID - p)
    sq = (f * f).astype(jnp.float32)
    tot = sq[:, None, None] + sq[None, :, None] + jnp.concatenate([sq, sq])[None, None, :]
    c = jnp.where(live, box_length**2 / (math.pi * GRID**3), 0.0)
    return jnp.where(tot > 0.5, c / jnp.maximum(tot, 1.0), 0.0)


def dot(a, b):
    return jnp.dot(a, b, preferred_element_type=jnp.float32)


def along_lanes(x, right):
    hi, lo = split(x)
    y = dot(jnp.concatenate([hi, lo], axis=1), right)
    return y[:, :128] + y[:, 128:]


def along_rows(left, x):
    hi, lo = split(x)
    return dot(left, jnp.concatenate([hi, lo, hi], axis=0))


def solve_kernel(first, seat_ref, row_ref, *refs):
    early_ref, late_ref, fourth_ref, other_early_ref, other_late_ref = refs[:5]
    left_ref, right_ref, green_ref = refs[5:8]
    col_ref, f_ref = refs[-2:]
    out_ref = refs[-3]
    group = seat_ref[0]
    core = jnp.bitwise_and(group, 1)
    z = jnp.bitwise_and(jnp.right_shift(group, 1), 7)

    def place(ref, start, holder, block):
        rows = pl.ds(pl.multiple_of(8 * jnp.bitwise_and(block + 8, 7), 8), 8)
        for i in range(2):
            col_ref[jnp.bitwise_xor(i, holder), rows, :] = ref[start + i].astype(jnp.float32)

    place(early_ref, 0, core, z)
    place(fourth_ref, 0, core, z + 4)
    sides = ((core, early_ref, late_ref), (1 - core, other_early_ref, other_late_ref))
    for holder, early, late in sides:
        sign = jnp.where(holder == 0, -1, 1)
        place(early, 2, holder, z + sign)
        place(late, 0, holder, z + 3 * sign)
        place(late, 2, holder, z + 2 * sign)

    left = left_ref[...]
    right = right_ref[...]
    low = lax.broadcasted_iota(jnp.int32, (GRID, 128), 1) < 64

    packed = []
    for i in range(32):
        lanes = slice(128 * i, 128 * i + 128)
        row = row_ref[:, lanes].astype(jnp.float32)
        d1 = row * col_ref[0, :, lanes]
        d2 = row * col_ref[1, :, lanes]
        packed.append(jnp.where(low, d1, pltpu.roll(d2, 64, 1)))
        packed.append(jnp.where(low, pltpu.roll(d1, 64, 1), d2))
    g = along_lanes(jnp.concatenate(packed, axis=0), right)
    wide = jnp.concatenate([g[64 * i : 64 * i + 64] for i in range(64)], axis=1)
    h = along_rows(left, wide)
    for i in range(64):
        f_ref[PITCH * i : PITCH * i + 64, :] = h[:, 128 * i : 128 * i + 128]

    def middle(step, _):
        kx = step * GM
        parts = [f_ref[pl.ds(kx + i, 64, stride=PITCH), :] for i in range(GM)]
        h = along_rows(left, jnp.concatenate(parts, axis=1))
        h = h * jnp.concatenate([green_ref[kx + i] for i in range(GM)], axis=1)
        u = along_rows(left, h)
        for i in range(GM):
            f_ref[pl.ds(kx + i, 64, stride=PITCH), :] = u[:, 128 * i : 128 * i + 128]
        return 0

    lax.fori_loop(0, 64 // GM, middle, 0)

    occ = [-col_ref[member, 0:1, 4096:4224] for member in range(2)]
    wide = jnp.concatenate([f_ref[PITCH * i : PITCH * i + 64, :] for i in range(64)], axis=1)
    g = along_rows(left, wide)
    tall = jnp.concatenate([g[:, 128 * i : 128 * i + 128] for i in range(64)], axis=0)
    p = along_lanes(tall, right)
    for i in range(32):
        lanes = slice(128 * i, 128 * i + 128)
        p0, p1 = p[128 * i : 128 * i + 64], p[128 * i + 64 : 128 * i + 128]
        v1 = jnp.where(low, p0, pltpu.roll(p1, 64, 1))
        v2 = jnp.where(low, pltpu.roll(p0, 64, 1), p1)
        term = v1 * (col_ref[0, :, lanes] * occ[0]) + v2 * (col_ref[1, :, lanes] * occ[1])
        if not first:
            term = refs[8][:, lanes] + term
        out_ref[:, lanes] = term

    if not first:
        level = jnp.zeros((GRID, 128), jnp.float32)
        for i in range(32):
            level = jnp.maximum(level, jnp.abs(out_ref[:, 128 * i : 128 * i + 128]))
        peak = jnp.maximum(jnp.max(level, axis=(0, 1), keepdims=True), 1e-30)
        power = jnp.ceil(jnp.log2(jnp.broadcast_to(peak, (8, 128)))) - 15.0
        factor = jnp.exp2(-power)[0:1]
        for i in range(32):
            lanes = slice(128 * i, 128 * i + 128)
            out_ref[:, lanes] = out_ref[:, lanes] * factor
        out_ref[:, 4096:4224] = jnp.broadcast_to(power[0:1], (GRID, 128))


def copies_kernel(x_ref, out_ref, sem):
    source = x_ref.at[:, : GRID * GRID]
    sends = [pltpu.make_async_copy(source, out_ref.at[i], sem.at[i]) for i in range(8)]
    for send in sends:
        send.start()
    for send in sends:
        send.wait()


def copies_of(x):
    return pl.pallas_call(
        copies_kernel,
        out_shape=jax.ShapeDtypeStruct((8, 8, GRID * GRID), x.dtype),
        in_specs=[pl.BlockSpec(memory_space=pltpu.VMEM)],
        out_specs=pl.BlockSpec(memory_space=pl.ANY),
        scratch_shapes=[pltpu.SemaphoreType.DMA((8,))],
        compiler_params=pltpu.CompilerParams(vmem_limit_bytes=2**20),
        name="copies",
    )(x)


def solve(seat, row, mine, other, left, right, green, *more):
    vm = pl.BlockSpec(memory_space=pltpu.VMEM)
    sm = pl.BlockSpec(memory_space=pltpu.SMEM)
    width = GRID * GRID + (128 if more else 0)
    return pl.pallas_call(
        functools.partial(solve_kernel, not more),
        out_shape=jax.ShapeDtypeStruct((GRID, width), jnp.float32),
        in_specs=[sm] + [vm] * (9 + len(more)),
        out_specs=vm,
        scratch_shapes=[
            pltpu.VMEM((2, GRID, GRID * GRID + 128), jnp.float32),
            pltpu.VMEM((GRID * PITCH, 128), jnp.float32),
        ],
        cost_estimate=pl.CostEstimate(flops=10**10, bytes_accessed=10**7, transcendentals=0),
        compiler_params=pltpu.CompilerParams(vmem_limit_bytes=32 * 2**20),
        name="solve",
    )(seat, row, *mine, *other, left, right, green, *more)


AXES = ("grp", "dist")


def device(half, z, core, lane):
    return ((half * 8 + z) * 2 + core) * 8 + lane


def moved(x, rule):
    pairs = [
        (device(h, z, c, l), device(*rule(h, z, c, l)))
        for h in range(2)
        for z in range(8)
        for c in range(2)
        for l in range(8)
    ]
    return lax.ppermute(x, AXES, pairs)


def body(orbitals, occupations):
    return exchange(orbitals[0], occupations[0])


def cores(h, z, c, l):
    return (h, z, 1 - c, l)


def halves(h, z, c, l):
    return (1 - h, z, c, l)


def ring(k):
    return lambda h, z, c, l: (h, (z + (k if c == 0 else 8 - k)) % 8, c, l)


def exchange(mine, occupation):
    slice_out = jnp.concatenate([mine, jnp.broadcast_to(occupation, (8, 128))], axis=1)
    kept = moved(slice_out, lambda h, z, c, l: (h, l, c, z))
    copies = copies_of(slice_out)
    row = lax.all_to_all(copies, "dist", split_axis=0, concat_axis=0, tiled=True)
    row = row.reshape(GRID, GRID * GRID)
    crossed = moved(kept, cores)
    seat = lax.axis_index("grp").astype(jnp.int32).reshape(1)
    pair, seat = lax.optimization_barrier((jnp.stack([kept, crossed]), seat))
    live = seat[0] >= 0
    left, right = tables()
    left = jnp.where(live, left, 0)
    right = jnp.where(live, right, 0)
    green = green_table(live)
    hop = {}
    for k in (1, 3, 2):
        hop[k] = moved(pair, ring(k))
    held, first, left, right, green = lax.optimization_barrier((pair, hop[1], left, right, green))
    early = jnp.concatenate([held, first])
    far_early = moved(early, halves)
    core_early = moved(early, cores)
    fourth = moved(jnp.where(live, hop[3], 0), ring(1))
    late = jnp.concatenate([hop[3], hop[2]])
    core_late = moved(late, cores)
    far_late = moved(late, halves)
    far_fourth = moved(fourth, halves)
    far_core_early = moved(far_early, cores)
    mine, other = (early, late, fourth), (core_early, core_late)
    partial = solve(seat, row, mine, other, left, right, green)
    far_late, partial = lax.optimization_barrier((far_late, partial))
    far_core_late = moved(far_late, cores)
    mine, other = (far_early, far_late, far_fourth), (far_core_early, far_core_late)
    partial = solve(seat, row, mine, other, left, right, green, partial)
    sent = partial.astype(jnp.float16).reshape(8, 8, GRID * GRID + 128)
    arrived = lax.all_to_all(sent, "dist", split_axis=0, concat_axis=0, tiled=True)
    power = lax.optimization_barrier(arrived[:, 0:1, GRID * GRID : GRID * GRID + 1])
    terms = arrived[:, :, : GRID * GRID].astype(jnp.float32) * jnp.exp2(power.astype(jnp.float32))
    return terms.sum(axis=0)[None]


def solution(mesh):
    in_specs = (P("grp", "dist", None), P("grp"))
    out_specs = P("grp", "dist", None)
    return jax.shard_map(body, mesh=mesh, in_specs=in_specs, out_specs=out_specs, check_vma=False)
```

```python
import functools
import math

import jax
import jax.numpy as jnp
import numpy as np
from jax import lax
from jax.experimental import pallas as pl
from jax.experimental.pallas import tpu as pltpu
from jax.sharding import PartitionSpec as P

GRID = 64
GM = 32
PITCH = 65
box_length = 7.0


def split(x):
    hi = x.astype(jnp.bfloat16)
    lo = (x - hi.astype(jnp.float32)).astype(jnp.bfloat16)
    return hi, lo


def tables():
    position = np.arange(GRID)
    angles = (position[:, None] * position[None, :] % GRID) * (2.0 * math.pi / GRID)
    t = np.cos(angles) + np.sin(angles)
    hi = t.astype(jnp.bfloat16)
    lo = (t - hi.astype(np.float64)).astype(jnp.bfloat16)
    hi, lo = jnp.asarray(hi), jnp.asarray(lo)
    left = jnp.concatenate([hi, hi, lo], axis=1)
    zero = jnp.zeros_like(hi)
    two = lambda m: jnp.concatenate([jnp.concatenate([m, zero], 1), jnp.concatenate([zero, m], 1)], 0)
    wide = jnp.concatenate([two(hi), two(lo)], axis=1)
    right = jnp.concatenate([wide, wide], axis=0)
    return left, right


def green_table(live):
    p = jnp.arange(GRID, dtype=jnp.int32)
    f = jnp.minimum(p, GRID - p)
    sq = (f * f).astype(jnp.float32)
    tot = sq[:, None, None] + sq[None, :, None] + jnp.concatenate([sq, sq])[None, None, :]
    c = jnp.where(live, box_length**2 / (math.pi * GRID**3), 0.0)
    return jnp.where(tot > 0.5, c / jnp.maximum(tot, 1.0), 0.0)


def dot(a, b):
    return jnp.dot(a, b, preferred_element_type=jnp.float32)


def along_lanes(x, right):
    hi, lo = split(x)
    y = dot(jnp.concatenate([hi, lo], axis=1), right)
    return y[:, :128] + y[:, 128:]


def along_rows(left, x):
    hi, lo = split(x)
    return dot(left, jnp.concatenate([hi, lo, hi], axis=0))


def solve_kernel(first, seat_ref, row_ref, *refs):
    early_ref, late_ref, fourth_ref, other_early_ref, other_late_ref = refs[:5]
    left_ref, right_ref, green_ref = refs[5:8]
    col_ref, f_ref = refs[-2:]
    out_ref = refs[-3]
    group = seat_ref[0]
    core = jnp.bitwise_and(group, 1)
    z = jnp.bitwise_and(jnp.right_shift(group, 1), 7)

    def place(ref, start, holder, block):
        rows = pl.ds(pl.multiple_of(8 * jnp.bitwise_and(block + 8, 7), 8), 8)
        for i in range(2):
            col_ref[jnp.bitwise_xor(i, holder), rows, :] = ref[start + i].astype(jnp.float32)

    place(early_ref, 0, core, z)
    place(fourth_ref, 0, core, z + 4)
    sides = ((core, early_ref, late_ref), (1 - core, other_early_ref, other_late_ref))
    for holder, early, late in sides:
        sign = jnp.where(holder == 0, -1, 1)
        place(early, 2, holder, z + 3 * sign)
        place(late, 0, holder, z + 2 * sign)
        place(late, 2, holder, z + sign)

    left = left_ref[...]
    right = right_ref[...]
    low = lax.broadcasted_iota(jnp.int32, (GRID, 128), 1) < 64

    packed = []
    for i in range(32):
        lanes = slice(128 * i, 128 * i + 128)
        row = row_ref[:, lanes].astype(jnp.float32)
        d1 = row * col_ref[0, :, lanes]
        d2 = row * col_ref[1, :, lanes]
        packed.append(jnp.where(low, d1, pltpu.roll(d2, 64, 1)))
        packed.append(jnp.where(low, pltpu.roll(d1, 64, 1), d2))
    g = along_lanes(jnp.concatenate(packed, axis=0), right)
    wide = jnp.concatenate([g[64 * i : 64 * i + 64] for i in range(64)], axis=1)
    h = along_rows(left, wide)
    for i in range(64):
        f_ref[PITCH * i : PITCH * i + 64, :] = h[:, 128 * i : 128 * i + 128]

    def middle(step, _):
        kx = step * GM
        parts = [f_ref[pl.ds(kx + i, 64, stride=PITCH), :] for i in range(GM)]
        h = along_rows(left, jnp.concatenate(parts, axis=1))
        h = h * jnp.concatenate([green_ref[kx + i] for i in range(GM)], axis=1)
        u = along_rows(left, h)
        for i in range(GM):
            f_ref[pl.ds(kx + i, 64, stride=PITCH), :] = u[:, 128 * i : 128 * i + 128]
        return 0

    lax.fori_loop(0, 64 // GM, middle, 0)

    occ = [-col_ref[member, 0:1, 4096:4224] for member in range(2)]
    wide = jnp.concatenate([f_ref[PITCH * i : PITCH * i + 64, :] for i in range(64)], axis=1)
    g = along_rows(left, wide)
    tall = jnp.concatenate([g[:, 128 * i : 128 * i + 128] for i in range(64)], axis=0)
    p = along_lanes(tall, right)
    for i in range(32):
        lanes = slice(128 * i, 128 * i + 128)
        p0, p1 = p[128 * i : 128 * i + 64], p[128 * i + 64 : 128 * i + 128]
        v1 = jnp.where(low, p0, pltpu.roll(p1, 64, 1))
        v2 = jnp.where(low, pltpu.roll(p0, 64, 1), p1)
        term = v1 * (col_ref[0, :, lanes] * occ[0]) + v2 * (col_ref[1, :, lanes] * occ[1])
        if not first:
            term = refs[8][:, lanes] + term
        out_ref[:, lanes] = term

    if not first:
        level = jnp.zeros((GRID, 128), jnp.float32)
        for i in range(32):
            level = jnp.maximum(level, jnp.abs(out_ref[:, 128 * i : 128 * i + 128]))
        peak = jnp.maximum(jnp.max(level, axis=(0, 1), keepdims=True), 1e-30)
        power = jnp.ceil(jnp.log2(jnp.broadcast_to(peak, (8, 128)))) - 15.0
        factor = jnp.exp2(-power)[0:1]
        for i in range(32):
            lanes = slice(128 * i, 128 * i + 128)
            out_ref[:, lanes] = out_ref[:, lanes] * factor
        out_ref[:, 4096:4224] = jnp.broadcast_to(power[0:1], (GRID, 128))


def copies_kernel(x_ref, out_ref, sem):
    source = x_ref.at[:, : GRID * GRID]
    sends = [pltpu.make_async_copy(source, out_ref.at[i], sem.at[i]) for i in range(8)]
    for send in sends:
        send.start()
    for send in sends:
        send.wait()


def copies_of(x):
    return pl.pallas_call(
        copies_kernel,
        out_shape=jax.ShapeDtypeStruct((8, 8, GRID * GRID), x.dtype),
        in_specs=[pl.BlockSpec(memory_space=pltpu.VMEM)],
        out_specs=pl.BlockSpec(memory_space=pl.ANY),
        scratch_shapes=[pltpu.SemaphoreType.DMA((8,))],
        compiler_params=pltpu.CompilerParams(vmem_limit_bytes=2**20),
        name="copies",
    )(x)


def solve(seat, row, mine, other, left, right, green, *more):
    vm = pl.BlockSpec(memory_space=pltpu.VMEM)
    sm = pl.BlockSpec(memory_space=pltpu.SMEM)
    width = GRID * GRID + (128 if more else 0)
    return pl.pallas_call(
        functools.partial(solve_kernel, not more),
        out_shape=jax.ShapeDtypeStruct((GRID, width), jnp.float32),
        in_specs=[sm] + [vm] * (9 + len(more)),
        out_specs=vm,
        scratch_shapes=[
            pltpu.VMEM((2, GRID, GRID * GRID + 128), jnp.float32),
            pltpu.VMEM((GRID * PITCH, 128), jnp.float32),
        ],
        cost_estimate=pl.CostEstimate(flops=10**10, bytes_accessed=10**7, transcendentals=0),
        compiler_params=pltpu.CompilerParams(vmem_limit_bytes=32 * 2**20),
        name="solve",
    )(seat, row, *mine, *other, left, right, green, *more)


AXES = ("grp", "dist")


def device(half, z, core, lane):
    return ((half * 8 + z) * 2 + core) * 8 + lane


def moved(x, rule):
    pairs = [
        (device(h, z, c, l), device(*rule(h, z, c, l)))
        for h in range(2)
        for z in range(8)
        for c in range(2)
        for l in range(8)
    ]
    return lax.ppermute(x, AXES, pairs)


def body(orbitals, occupations):
    return exchange(orbitals[0], occupations[0])


def cores(h, z, c, l):
    return (h, z, 1 - c, l)


def halves(h, z, c, l):
    return (1 - h, z, c, l)


def ring(k):
    return lambda h, z, c, l: (h, (z + (k if c == 0 else 8 - k)) % 8, c, l)


def exchange(mine, occupation):
    slice_out = jnp.concatenate([mine, jnp.broadcast_to(occupation, (8, 128))], axis=1)
    kept = moved(slice_out, lambda h, z, c, l: (h, l, c, z))
    copies = copies_of(slice_out)
    row = lax.all_to_all(copies, "dist", split_axis=0, concat_axis=0, tiled=True)
    row = row.reshape(GRID, GRID * GRID)
    crossed = moved(kept, cores)
    seat = lax.axis_index("grp").astype(jnp.int32).reshape(1)
    pair, seat = lax.optimization_barrier((jnp.stack([kept, crossed]), seat))
    live = seat[0] >= 0
    left, right = tables()
    left = jnp.where(live, left, 0)
    right = jnp.where(live, right, 0)
    green = green_table(live)
    hop = {}
    for k in (3, 2, 1):
        hop[k] = moved(pair, ring(k))
    fourth = moved(jnp.where(live, hop[3], 0), ring(1))
    held, third, left, right, green = lax.optimization_barrier((pair, hop[3], left, right, green))
    early = jnp.concatenate([held, third])
    far_early = moved(early, halves)
    core_early = moved(early, cores)
    late = jnp.concatenate([hop[2], hop[1]])
    core_late = moved(late, cores)
    far_late = moved(late, halves)
    far_fourth = moved(fourth, halves)
    far_core_early = moved(far_early, cores)
    mine, other = (early, late, fourth), (core_early, core_late)
    partial = solve(seat, row, mine, other, left, right, green)
    far_late, partial = lax.optimization_barrier((far_late, partial))
    far_core_late = moved(far_late, cores)
    mine, other = (far_early, far_late, far_fourth), (far_core_early, far_core_late)
    partial = solve(seat, row, mine, other, left, right, green, partial)
    sent = partial.astype(jnp.float16).reshape(8, 8, GRID * GRID + 128)
    arrived = lax.all_to_all(sent, "dist", split_axis=0, concat_axis=0, tiled=True)
    power = lax.optimization_barrier(arrived[:, 0:1, GRID * GRID : GRID * GRID + 1])
    terms = arrived[:, :, : GRID * GRID].astype(jnp.float32) * jnp.exp2(power.astype(jnp.float32))
    return terms.sum(axis=0)[None]


def solution(mesh):
    in_specs = (P("grp", "dist", None), P("grp"))
    out_specs = P("grp", "dist", None)
    return jax.shard_map(body, mesh=mesh, in_specs=in_specs, out_specs=out_specs, check_vma=False)
```

```python
import functools
import math

import jax
import jax.numpy as jnp
import numpy as np
from jax import lax
from jax.experimental import pallas as pl
from jax.experimental.pallas import tpu as pltpu
from jax.sharding import PartitionSpec as P

GRID = 64
GM = 32
PITCH = 65
box_length = 7.0


def split(x):
    hi = x.astype(jnp.bfloat16)
    lo = (x - hi.astype(jnp.float32)).astype(jnp.bfloat16)
    return hi, lo


def tables():
    position = np.arange(GRID)
    angles = (position[:, None] * position[None, :] % GRID) * (2.0 * math.pi / GRID)
    t = np.cos(angles) + np.sin(angles)
    hi = t.astype(jnp.bfloat16)
    lo = (t - hi.astype(np.float64)).astype(jnp.bfloat16)
    hi, lo = jnp.asarray(hi), jnp.asarray(lo)
    left = jnp.concatenate([hi, hi, lo], axis=1)
    zero = jnp.zeros_like(hi)
    two = lambda m: jnp.concatenate([jnp.concatenate([m, zero], 1), jnp.concatenate([zero, m], 1)], 0)
    wide = jnp.concatenate([two(hi), two(lo)], axis=1)
    right = jnp.concatenate([wide, wide], axis=0)
    return left, right


def green_table(live):
    p = jnp.arange(GRID, dtype=jnp.int32)
    f = jnp.minimum(p, GRID - p)
    sq = (f * f).astype(jnp.float32)
    tot = sq[: GRID // 2 + 1, None, None] + sq[None, :, None] + jnp.concatenate([sq, sq])[None, None, :]
    c = jnp.where(live, box_length**2 / (math.pi * GRID**3), 0.0)
    return jnp.where(tot > 0.5, c / jnp.maximum(tot, 1.0), 0.0)


def dot(a, b):
    return jnp.dot(a, b, preferred_element_type=jnp.float32)


def along_lanes(x, right):
    hi, lo = split(x)
    y = dot(jnp.concatenate([hi, lo], axis=1), right)
    return y[:, :128] + y[:, 128:]


def along_rows(left, x):
    hi, lo = split(x)
    return dot(left, jnp.concatenate([hi, lo, hi], axis=0))


def solve_kernel(first, seat_ref, row_ref, *refs):
    early_ref, late_ref, fourth_ref, other_early_ref, other_late_ref = refs[:5]
    left_ref, right_ref, green_ref = refs[5:8]
    col_ref, f_ref = refs[-2:]
    out_ref = refs[-3]
    group = seat_ref[0]
    core = jnp.bitwise_and(group, 1)
    z = jnp.bitwise_and(jnp.right_shift(group, 1), 7)

    def place(ref, start, holder, block):
        rows = pl.ds(pl.multiple_of(8 * jnp.bitwise_and(block + 8, 7), 8), 8)
        for i in range(2):
            col_ref[jnp.bitwise_xor(i, holder), rows, :] = ref[start + i].astype(jnp.float32)

    place(early_ref, 0, core, z)
    place(fourth_ref, 0, core, z + 4)
    sides = ((core, early_ref, late_ref), (1 - core, other_early_ref, other_late_ref))
    for holder, early, late in sides:
        sign = jnp.where(holder == 0, -1, 1)
        place(early, 2, holder, z + sign)
        place(late, 0, holder, z + 3 * sign)
        place(late, 2, holder, z + 2 * sign)

    left = left_ref[...]
    right = right_ref[...]
    low = lax.broadcasted_iota(jnp.int32, (GRID, 128), 1) < 64

    packed = []
    for i in range(32):
        lanes = slice(128 * i, 128 * i + 128)
        row = row_ref[:, lanes].astype(jnp.float32)
        d1 = row * col_ref[0, :, lanes]
        d2 = row * col_ref[1, :, lanes]
        packed.append(jnp.where(low, d1, pltpu.roll(d2, 64, 1)))
        packed.append(jnp.where(low, pltpu.roll(d1, 64, 1), d2))
    g = along_lanes(jnp.concatenate(packed, axis=0), right)
    wide = jnp.concatenate([g[64 * i : 64 * i + 64] for i in range(64)], axis=1)
    h = along_rows(left, wide)
    for i in range(64):
        f_ref[PITCH * i : PITCH * i + 64, :] = h[:, 128 * i : 128 * i + 128]

    def middle(step, _):
        kx = step * GM
        parts = [f_ref[pl.ds(kx + i, 64, stride=PITCH), :] for i in range(GM)]
        h = along_rows(left, jnp.concatenate(parts, axis=1))
        folded = [jnp.minimum(kx + i, GRID - kx - i) for i in range(GM)]
        h = h * jnp.concatenate([green_ref[k] for k in folded], axis=1)
        u = along_rows(left, h)
        for i in range(GM):
            f_ref[pl.ds(kx + i, 64, stride=PITCH), :] = u[:, 128 * i : 128 * i + 128]
        return 0

    lax.fori_loop(0, 64 // GM, middle, 0)

    occ = [-col_ref[member, 0:1, 4096:4224] for member in range(2)]
    wide = jnp.concatenate([f_ref[PITCH * i : PITCH * i + 64, :] for i in range(64)], axis=1)
    g = along_rows(left, wide)
    tall = jnp.concatenate([g[:, 128 * i : 128 * i + 128] for i in range(64)], axis=0)
    p = along_lanes(tall, right)
    for i in range(32):
        lanes = slice(128 * i, 128 * i + 128)
        p0, p1 = p[128 * i : 128 * i + 64], p[128 * i + 64 : 128 * i + 128]
        v1 = jnp.where(low, p0, pltpu.roll(p1, 64, 1))
        v2 = jnp.where(low, pltpu.roll(p0, 64, 1), p1)
        term = v1 * (col_ref[0, :, lanes] * occ[0]) + v2 * (col_ref[1, :, lanes] * occ[1])
        if not first:
            term = refs[8][:, lanes] + term
        out_ref[:, lanes] = term

    if not first:
        level = jnp.zeros((GRID, 128), jnp.float32)
        for i in range(32):
            level = jnp.maximum(level, jnp.abs(out_ref[:, 128 * i : 128 * i + 128]))
        peak = jnp.maximum(jnp.max(level, axis=(0, 1), keepdims=True), 1e-30)
        power = jnp.ceil(jnp.log2(jnp.broadcast_to(peak, (8, 128)))) - 15.0
        factor = jnp.exp2(-power)[0:1]
        for i in range(32):
            lanes = slice(128 * i, 128 * i + 128)
            out_ref[:, lanes] = out_ref[:, lanes] * factor
        out_ref[:, 4096:4224] = jnp.broadcast_to(power[0:1], (GRID, 128))


def copies_kernel(x_ref, out_ref, sem):
    source = x_ref.at[:, : GRID * GRID]
    sends = [pltpu.make_async_copy(source, out_ref.at[i], sem.at[i]) for i in range(8)]
    for send in sends:
        send.start()
    for send in sends:
        send.wait()


def copies_of(x):
    return pl.pallas_call(
        copies_kernel,
        out_shape=jax.ShapeDtypeStruct((8, 8, GRID * GRID), x.dtype),
        in_specs=[pl.BlockSpec(memory_space=pltpu.VMEM)],
        out_specs=pl.BlockSpec(memory_space=pl.ANY),
        scratch_shapes=[pltpu.SemaphoreType.DMA((8,))],
        compiler_params=pltpu.CompilerParams(vmem_limit_bytes=2**20),
        name="copies",
    )(x)


def solve(seat, row, mine, other, left, right, green, *more):
    vm = pl.BlockSpec(memory_space=pltpu.VMEM)
    sm = pl.BlockSpec(memory_space=pltpu.SMEM)
    width = GRID * GRID + (128 if more else 0)
    return pl.pallas_call(
        functools.partial(solve_kernel, not more),
        out_shape=jax.ShapeDtypeStruct((GRID, width), jnp.float32),
        in_specs=[sm] + [vm] * (9 + len(more)),
        out_specs=vm,
        scratch_shapes=[
            pltpu.VMEM((2, GRID, GRID * GRID + 128), jnp.float32),
            pltpu.VMEM((GRID * PITCH, 128), jnp.float32),
        ],
        cost_estimate=pl.CostEstimate(flops=10**10, bytes_accessed=10**7, transcendentals=0),
        compiler_params=pltpu.CompilerParams(vmem_limit_bytes=32 * 2**20),
        name="solve",
    )(seat, row, *mine, *other, left, right, green, *more)


AXES = ("grp", "dist")


def device(half, z, core, lane):
    return ((half * 8 + z) * 2 + core) * 8 + lane


def moved(x, rule):
    pairs = [
        (device(h, z, c, l), device(*rule(h, z, c, l)))
        for h in range(2)
        for z in range(8)
        for c in range(2)
        for l in range(8)
    ]
    return lax.ppermute(x, AXES, pairs)


def body(orbitals, occupations):
    return exchange(orbitals[0], occupations[0])


def cores(h, z, c, l):
    return (h, z, 1 - c, l)


def halves(h, z, c, l):
    return (1 - h, z, c, l)


def ring(k):
    return lambda h, z, c, l: (h, (z + (k if c == 0 else 8 - k)) % 8, c, l)


def exchange(mine, occupation):
    slice_out = jnp.concatenate([mine, jnp.broadcast_to(occupation, (8, 128))], axis=1)
    kept = moved(slice_out, lambda h, z, c, l: (h, l, c, z))
    copies = copies_of(slice_out)
    row = lax.all_to_all(copies, "dist", split_axis=0, concat_axis=0, tiled=True)
    row = row.reshape(GRID, GRID * GRID)
    crossed = moved(kept, cores)
    seat = lax.axis_index("grp").astype(jnp.int32).reshape(1)
    pair, seat = lax.optimization_barrier((jnp.stack([kept, crossed]), seat))
    live = seat[0] >= 0
    left, right = tables()
    left = jnp.where(live, left, 0)
    right = jnp.where(live, right, 0)
    green = green_table(live)
    hop = {}
    for k in (3, 1, 2):
        hop[k] = moved(pair, ring(k))
    held, first, left, right, green = lax.optimization_barrier((pair, hop[1], left, right, green))
    early = jnp.concatenate([held, first])
    far_early = moved(early, halves)
    core_early = moved(early, cores)
    fourth = moved(jnp.where(live, hop[3], 0), ring(1))
    late = jnp.concatenate([hop[3], hop[2]])
    core_late = moved(late, cores)
    far_late = moved(late, halves)
    far_fourth = moved(fourth, halves)
    far_core_early = moved(far_early, cores)
    mine, other = (early, late, fourth), (core_early, core_late)
    partial = solve(seat, row, mine, other, left, right, green)
    far_late, partial = lax.optimization_barrier((far_late, partial))
    far_core_late = moved(far_late, cores)
    mine, other = (far_early, far_late, far_fourth), (far_core_early, far_core_late)
    partial = solve(seat, row, mine, other, left, right, green, partial)
    sent = partial.astype(jnp.float16).reshape(8, 8, GRID * GRID + 128)
    arrived = lax.all_to_all(sent, "dist", split_axis=0, concat_axis=0, tiled=True)
    power = lax.optimization_barrier(arrived[:, 0:1, GRID * GRID : GRID * GRID + 1])
    terms = arrived[:, :, : GRID * GRID].astype(jnp.float32) * jnp.exp2(power.astype(jnp.float32))
    return terms.sum(axis=0)[None]


def solution(mesh):
    in_specs = (P("grp", "dist", None), P("grp"))
    out_specs = P("grp", "dist", None)
    return jax.shard_map(body, mesh=mesh, in_specs=in_specs, out_specs=out_specs, check_vma=False)
```

```python
import functools
import math

import jax
import jax.numpy as jnp
import numpy as np
from jax import lax
from jax.experimental import pallas as pl
from jax.experimental.pallas import tpu as pltpu
from jax.sharding import PartitionSpec as P

GRID = 64
GM = 32
PITCH = 65
box_length = 7.0


def split(x):
    hi = x.astype(jnp.bfloat16)
    lo = (x - hi.astype(jnp.float32)).astype(jnp.bfloat16)
    return hi, lo


def tables():
    position = np.arange(GRID)
    angles = (position[:, None] * position[None, :] % GRID) * (2.0 * math.pi / GRID)
    t = np.cos(angles) + np.sin(angles)
    hi = t.astype(jnp.bfloat16)
    lo = (t - hi.astype(np.float64)).astype(jnp.bfloat16)
    hi, lo = jnp.asarray(hi), jnp.asarray(lo)
    left = jnp.concatenate([hi, hi, lo], axis=1)
    zero = jnp.zeros_like(hi)
    two = lambda m: jnp.concatenate([jnp.concatenate([m, zero], 1), jnp.concatenate([zero, m], 1)], 0)
    wide = jnp.concatenate([two(hi), two(lo)], axis=1)
    right = jnp.concatenate([wide, wide], axis=0)
    return left, right


def green_table(live):
    p = jnp.arange(GRID, dtype=jnp.int32)
    f = jnp.minimum(p, GRID - p)
    sq = (f * f).astype(jnp.float32)
    tot = sq[: GRID // 2 + 1, None, None] + sq[None, :, None] + jnp.concatenate([sq, sq])[None, None, :]
    c = jnp.where(live, box_length**2 / (math.pi * GRID**3), 0.0)
    return jnp.where(tot > 0.5, c / jnp.maximum(tot, 1.0), 0.0)


def dot(a, b):
    return jnp.dot(a, b, preferred_element_type=jnp.float32)


def along_lanes(x, right):
    hi, lo = split(x)
    y = dot(jnp.concatenate([hi, lo], axis=1), right)
    return y[:, :128] + y[:, 128:]


def along_rows(left, x):
    hi, lo = split(x)
    return dot(left, jnp.concatenate([hi, lo, hi], axis=0))


def solve_kernel(first, seat_ref, row_ref, *refs):
    early_ref, late_ref, fourth_ref, other_early_ref, other_late_ref = refs[:5]
    left_ref, right_ref, green_ref = refs[5:8]
    col_ref, f_ref = refs[-2:]
    out_ref = refs[-3]
    group = seat_ref[0]
    core = jnp.bitwise_and(group, 1)
    z = jnp.bitwise_and(jnp.right_shift(group, 1), 7)

    def place(ref, start, holder, block):
        rows = pl.ds(pl.multiple_of(8 * jnp.bitwise_and(block + 8, 7), 8), 8)
        for i in range(2):
            col_ref[jnp.bitwise_xor(i, holder), rows, :] = ref[start + i].astype(jnp.float32)

    place(early_ref, 0, core, z)
    place(fourth_ref, 0, core, z + 4)
    sides = ((core, early_ref, 2, late_ref), (1 - core, other_early_ref, 0, other_late_ref))
    for holder, early, start, late in sides:
        sign = jnp.where(holder == 0, -1, 1)
        place(early, start, holder, z + sign)
        place(late, 0, holder, z + 3 * sign)
        place(late, 2, holder, z + 2 * sign)

    left = left_ref[...]
    right = right_ref[...]
    low = lax.broadcasted_iota(jnp.int32, (GRID, 128), 1) < 64

    packed = []
    for i in range(32):
        lanes = slice(128 * i, 128 * i + 128)
        row = row_ref[:, lanes].astype(jnp.float32)
        d1 = row * col_ref[0, :, lanes]
        d2 = row * col_ref[1, :, lanes]
        packed.append(jnp.where(low, d1, pltpu.roll(d2, 64, 1)))
        packed.append(jnp.where(low, pltpu.roll(d1, 64, 1), d2))
    g = along_lanes(jnp.concatenate(packed, axis=0), right)
    wide = jnp.concatenate([g[64 * i : 64 * i + 64] for i in range(64)], axis=1)
    h = along_rows(left, wide)
    for i in range(64):
        f_ref[PITCH * i : PITCH * i + 64, :] = h[:, 128 * i : 128 * i + 128]

    def middle(step, _):
        kx = step * GM
        parts = [f_ref[pl.ds(kx + i, 64, stride=PITCH), :] for i in range(GM)]
        h = along_rows(left, jnp.concatenate(parts, axis=1))
        folded = [jnp.minimum(kx + i, GRID - kx - i) for i in range(GM)]
        h = h * jnp.concatenate([green_ref[k] for k in folded], axis=1)
        u = along_rows(left, h)
        for i in range(GM):
            f_ref[pl.ds(kx + i, 64, stride=PITCH), :] = u[:, 128 * i : 128 * i + 128]
        return 0

    lax.fori_loop(0, 64 // GM, middle, 0)

    occ = [-col_ref[member, 0:1, 4096:4224] for member in range(2)]
    wide = jnp.concatenate([f_ref[PITCH * i : PITCH * i + 64, :] for i in range(64)], axis=1)
    g = along_rows(left, wide)
    tall = jnp.concatenate([g[:, 128 * i : 128 * i + 128] for i in range(64)], axis=0)
    p = along_lanes(tall, right)
    for i in range(32):
        lanes = slice(128 * i, 128 * i + 128)
        p0, p1 = p[128 * i : 128 * i + 64], p[128 * i + 64 : 128 * i + 128]
        v1 = jnp.where(low, p0, pltpu.roll(p1, 64, 1))
        v2 = jnp.where(low, pltpu.roll(p0, 64, 1), p1)
        term = v1 * (col_ref[0, :, lanes] * occ[0]) + v2 * (col_ref[1, :, lanes] * occ[1])
        if not first:
            term = refs[8][:, lanes] + term
        out_ref[:, lanes] = term

    if not first:
        level = jnp.zeros((GRID, 128), jnp.float32)
        for i in range(32):
            level = jnp.maximum(level, jnp.abs(out_ref[:, 128 * i : 128 * i + 128]))
        peak = jnp.maximum(jnp.max(level, axis=(0, 1), keepdims=True), 1e-30)
        power = jnp.ceil(jnp.log2(jnp.broadcast_to(peak, (8, 128)))) - 15.0
        factor = jnp.exp2(-power)[0:1]
        for i in range(32):
            lanes = slice(128 * i, 128 * i + 128)
            out_ref[:, lanes] = out_ref[:, lanes] * factor
        out_ref[:, 4096:4224] = jnp.broadcast_to(power[0:1], (GRID, 128))


def copies_kernel(x_ref, out_ref, sem):
    source = x_ref.at[:, : GRID * GRID]
    sends = [pltpu.make_async_copy(source, out_ref.at[i], sem.at[i]) for i in range(8)]
    for send in sends:
        send.start()
    for send in sends:
        send.wait()


def copies_of(x):
    return pl.pallas_call(
        copies_kernel,
        out_shape=jax.ShapeDtypeStruct((8, 8, GRID * GRID), x.dtype),
        in_specs=[pl.BlockSpec(memory_space=pltpu.VMEM)],
        out_specs=pl.BlockSpec(memory_space=pl.ANY),
        scratch_shapes=[pltpu.SemaphoreType.DMA((8,))],
        compiler_params=pltpu.CompilerParams(vmem_limit_bytes=2**20),
        name="copies",
    )(x)


def solve(seat, row, mine, other, left, right, green, *more):
    vm = pl.BlockSpec(memory_space=pltpu.VMEM)
    sm = pl.BlockSpec(memory_space=pltpu.SMEM)
    width = GRID * GRID + (128 if more else 0)
    return pl.pallas_call(
        functools.partial(solve_kernel, not more),
        out_shape=jax.ShapeDtypeStruct((GRID, width), jnp.float32),
        in_specs=[sm] + [vm] * (9 + len(more)),
        out_specs=vm,
        scratch_shapes=[
            pltpu.VMEM((2, GRID, GRID * GRID + 128), jnp.float32),
            pltpu.VMEM((GRID * PITCH, 128), jnp.float32),
        ],
        cost_estimate=pl.CostEstimate(flops=10**10, bytes_accessed=10**7, transcendentals=0),
        compiler_params=pltpu.CompilerParams(vmem_limit_bytes=32 * 2**20),
        name="solve",
    )(seat, row, *mine, *other, left, right, green, *more)


AXES = ("grp", "dist")


def device(half, z, core, lane):
    return ((half * 8 + z) * 2 + core) * 8 + lane


def moved(x, rule):
    pairs = [
        (device(h, z, c, l), device(*rule(h, z, c, l)))
        for h in range(2)
        for z in range(8)
        for c in range(2)
        for l in range(8)
    ]
    return lax.ppermute(x, AXES, pairs)


def body(orbitals, occupations):
    return exchange(orbitals[0], occupations[0])


def cores(h, z, c, l):
    return (h, z, 1 - c, l)


def halves(h, z, c, l):
    return (1 - h, z, c, l)


def ring(k):
    return lambda h, z, c, l: (h, (z + (k if c == 0 else 8 - k)) % 8, c, l)


def exchange(mine, occupation):
    slice_out = jnp.concatenate([mine, jnp.broadcast_to(occupation, (8, 128))], axis=1)
    kept = moved(slice_out, lambda h, z, c, l: (h, l, c, z))
    copies = copies_of(slice_out)
    row = lax.all_to_all(copies, "dist", split_axis=0, concat_axis=0, tiled=True)
    row = row.reshape(GRID, GRID * GRID)
    crossed = moved(kept, cores)
    seat = lax.axis_index("grp").astype(jnp.int32).reshape(1)
    pair, seat = lax.optimization_barrier((jnp.stack([kept, crossed]), seat))
    live = seat[0] >= 0
    left, right = tables()
    left = jnp.where(live, left, 0)
    right = jnp.where(live, right, 0)
    green = green_table(live)
    hop = {}
    for k in (1, 3, 2):
        hop[k] = moved(pair, ring(k))
    held, first, left, right, green = lax.optimization_barrier((pair, hop[1], left, right, green))
    early = jnp.concatenate([held, first])
    far_early = moved(early, halves)
    core_early = moved(first, cores)
    fourth = moved(jnp.where(live, hop[3], 0), ring(1))
    late = jnp.concatenate([hop[3], hop[2]])
    core_late = moved(late, cores)
    far_late = moved(late, halves)
    far_fourth = moved(fourth, halves)
    mine, other = (early, late, fourth), (core_early, core_late)
    partial = solve(seat, row, mine, other, left, right, green)
    far_early, far_late, partial = lax.optimization_barrier((far_early, far_late, partial))
    far_core_early = moved(far_early[2:], cores)
    far_core_late = moved(far_late, cores)
    mine, other = (far_early, far_late, far_fourth), (far_core_early, far_core_late)
    partial = solve(seat, row, mine, other, left, right, green, partial)
    sent = partial.astype(jnp.float16).reshape(8, 8, GRID * GRID + 128)
    arrived = lax.all_to_all(sent, "dist", split_axis=0, concat_axis=0, tiled=True)
    power = lax.optimization_barrier(arrived[:, 0:1, GRID * GRID : GRID * GRID + 1])
    terms = arrived[:, :, : GRID * GRID].astype(jnp.float32) * jnp.exp2(power.astype(jnp.float32))
    return terms.sum(axis=0)[None]


def solution(mesh):
    in_specs = (P("grp", "dist", None), P("grp"))
    out_specs = P("grp", "dist", None)
    return jax.shard_map(body, mesh=mesh, in_specs=in_specs, out_specs=out_specs, check_vma=False)
```

```python
import functools
import math

import jax
import jax.numpy as jnp
import numpy as np
from jax import lax
from jax.experimental import pallas as pl
from jax.experimental.pallas import tpu as pltpu
from jax.sharding import PartitionSpec as P

GRID = 64
GM = 32
PITCH = 65
box_length = 7.0


def split(x):
    hi = x.astype(jnp.bfloat16)
    lo = (x - hi.astype(jnp.float32)).astype(jnp.bfloat16)
    return hi, lo


def tables():
    position = np.arange(GRID)
    angles = (position[:, None] * position[None, :] % GRID) * (2.0 * math.pi / GRID)
    t = np.cos(angles) + np.sin(angles)
    hi = t.astype(jnp.bfloat16)
    lo = (t - hi.astype(np.float64)).astype(jnp.bfloat16)
    hi, lo = jnp.asarray(hi), jnp.asarray(lo)
    left = jnp.concatenate([hi, hi, lo], axis=1)
    zero = jnp.zeros_like(hi)
    two = lambda m: jnp.concatenate([jnp.concatenate([m, zero], 1), jnp.concatenate([zero, m], 1)], 0)
    wide = jnp.concatenate([two(hi), two(lo)], axis=1)
    right = jnp.concatenate([wide, wide], axis=0)
    return left, right


def green_table(live):
    p = jnp.arange(GRID, dtype=jnp.int32)
    f = jnp.minimum(p, GRID - p)
    sq = (f * f).astype(jnp.float32)
    tot = sq[: GRID // 2 + 1, None, None] + sq[None, :, None] + jnp.concatenate([sq, sq])[None, None, :]
    c = jnp.where(live, box_length**2 / (math.pi * GRID**3), 0.0)
    return jnp.where(tot > 0.5, c / jnp.maximum(tot, 1.0), 0.0)


def dot(a, b):
    return jnp.dot(a, b, preferred_element_type=jnp.float32)


def along_lanes(x, right):
    hi, lo = split(x)
    y = dot(jnp.concatenate([hi, lo], axis=1), right)
    return y[:, :128] + y[:, 128:]


def along_rows(left, x):
    hi, lo = split(x)
    return dot(left, jnp.concatenate([hi, lo, hi], axis=0))


def solve_kernel(first, seat_ref, row_ref, *refs):
    early_ref, late_ref, fourth_ref, other_early_ref, other_late_ref = refs[:5]
    left_ref, right_ref, green_ref = refs[5:8]
    col_ref, f_ref = refs[-2:]
    out_ref = refs[-3]
    group = seat_ref[0]
    core = jnp.bitwise_and(group, 1)
    z = jnp.bitwise_and(jnp.right_shift(group, 1), 7)

    def place(ref, start, holder, block):
        rows = pl.ds(pl.multiple_of(8 * jnp.bitwise_and(block + 8, 7), 8), 8)
        for i in range(2):
            col_ref[jnp.bitwise_xor(i, holder), rows, :] = ref[start + i].astype(jnp.float32)

    place(early_ref, 0, core, z)
    place(fourth_ref, 0, core, z + 4)
    sides = ((core, early_ref, 2, late_ref), (1 - core, other_early_ref, 0, other_late_ref))
    for holder, early, start, late in sides:
        sign = jnp.where(holder == 0, -1, 1)
        place(early, start, holder, z + sign)
        place(late, 0, holder, z + 3 * sign)
        place(late, 2, holder, z + 2 * sign)

    left = left_ref[...]
    right = right_ref[...]
    low = lax.broadcasted_iota(jnp.int32, (GRID, 128), 1) < 64

    packed = []
    for i in range(32):
        lanes = slice(128 * i, 128 * i + 128)
        row = row_ref[:, lanes].astype(jnp.float32)
        d1 = row * col_ref[0, :, lanes]
        d2 = row * col_ref[1, :, lanes]
        packed.append(jnp.where(low, d1, pltpu.roll(d2, 64, 1)))
        packed.append(jnp.where(low, pltpu.roll(d1, 64, 1), d2))
    g = along_lanes(jnp.concatenate(packed, axis=0), right)
    wide = jnp.concatenate([g[64 * i : 64 * i + 64] for i in range(64)], axis=1)
    h = along_rows(left, wide)
    for i in range(64):
        f_ref[PITCH * i : PITCH * i + 64, :] = h[:, 128 * i : 128 * i + 128]

    def middle(step, _):
        kx = step * GM
        parts = [f_ref[pl.ds(kx + i, 64, stride=PITCH), :] for i in range(GM)]
        h = along_rows(left, jnp.concatenate(parts, axis=1))
        folded = [jnp.minimum(kx + i, GRID - kx - i) for i in range(GM)]
        h = h * jnp.concatenate([green_ref[k] for k in folded], axis=1)
        u = along_rows(left, h)
        for i in range(GM):
            f_ref[pl.ds(kx + i, 64, stride=PITCH), :] = u[:, 128 * i : 128 * i + 128]
        return 0

    lax.fori_loop(0, 64 // GM, middle, 0)

    occ = [-col_ref[member, 0:1, 4096:4224] for member in range(2)]
    wide = jnp.concatenate([f_ref[PITCH * i : PITCH * i + 64, :] for i in range(64)], axis=1)
    g = along_rows(left, wide)
    tall = jnp.concatenate([g[:, 128 * i : 128 * i + 128] for i in range(64)], axis=0)
    p = along_lanes(tall, right)
    for i in range(32):
        lanes = slice(128 * i, 128 * i + 128)
        p0, p1 = p[128 * i : 128 * i + 64], p[128 * i + 64 : 128 * i + 128]
        v1 = jnp.where(low, p0, pltpu.roll(p1, 64, 1))
        v2 = jnp.where(low, pltpu.roll(p0, 64, 1), p1)
        term = v1 * (col_ref[0, :, lanes] * occ[0]) + v2 * (col_ref[1, :, lanes] * occ[1])
        if not first:
            term = refs[8][:, lanes] + term
        out_ref[:, lanes] = term

    if not first:
        level = jnp.zeros((GRID, 128), jnp.float32)
        for i in range(32):
            level = jnp.maximum(level, jnp.abs(out_ref[:, 128 * i : 128 * i + 128]))
        peak = jnp.maximum(jnp.max(level, axis=(0, 1), keepdims=True), 1e-30)
        power = jnp.ceil(jnp.log2(jnp.broadcast_to(peak, (8, 128)))) - 15.0
        factor = jnp.exp2(-power)[0:1]
        for i in range(32):
            lanes = slice(128 * i, 128 * i + 128)
            out_ref[:, lanes] = out_ref[:, lanes] * factor
        out_ref[:, 4096:4224] = jnp.broadcast_to(power[0:1], (GRID, 128))


def copies_kernel(x_ref, out_ref, sem):
    source = x_ref.at[:, : GRID * GRID]
    sends = [pltpu.make_async_copy(source, out_ref.at[i], sem.at[i]) for i in range(8)]
    for send in sends:
        send.start()
    for send in sends:
        send.wait()


def copies_of(x):
    return pl.pallas_call(
        copies_kernel,
        out_shape=jax.ShapeDtypeStruct((8, 8, GRID * GRID), x.dtype),
        in_specs=[pl.BlockSpec(memory_space=pltpu.VMEM)],
        out_specs=pl.BlockSpec(memory_space=pl.ANY),
        scratch_shapes=[pltpu.SemaphoreType.DMA((8,))],
        compiler_params=pltpu.CompilerParams(vmem_limit_bytes=2**20),
        name="copies",
    )(x)


def solve(seat, row, mine, other, left, right, green, *more):
    vm = pl.BlockSpec(memory_space=pltpu.VMEM)
    sm = pl.BlockSpec(memory_space=pltpu.SMEM)
    width = GRID * GRID + (128 if more else 0)
    return pl.pallas_call(
        functools.partial(solve_kernel, not more),
        out_shape=jax.ShapeDtypeStruct((GRID, width), jnp.float32),
        in_specs=[sm] + [vm] * (9 + len(more)),
        out_specs=vm,
        scratch_shapes=[
            pltpu.VMEM((2, GRID, GRID * GRID + 128), jnp.float32),
            pltpu.VMEM((GRID * PITCH, 128), jnp.float32),
        ],
        cost_estimate=pl.CostEstimate(flops=10**10, bytes_accessed=10**7, transcendentals=0),
        compiler_params=pltpu.CompilerParams(vmem_limit_bytes=32 * 2**20),
        name="solve",
    )(seat, row, *mine, *other, left, right, green, *more)


AXES = ("grp", "dist")


def device(half, z, core, lane):
    return ((half * 8 + z) * 2 + core) * 8 + lane


def moved(x, rule):
    pairs = [
        (device(h, z, c, l), device(*rule(h, z, c, l)))
        for h in range(2)
        for z in range(8)
        for c in range(2)
        for l in range(8)
    ]
    return lax.ppermute(x, AXES, pairs)


def body(orbitals, occupations):
    return exchange(orbitals[0], occupations[0])


def cores(h, z, c, l):
    return (h, z, 1 - c, l)


def halves(h, z, c, l):
    return (1 - h, z, c, l)


def ring(k):
    return lambda h, z, c, l: (h, (z + (k if c == 0 else 8 - k)) % 8, c, l)


def exchange(mine, occupation):
    slice_out = jnp.concatenate([mine, jnp.broadcast_to(occupation, (8, 128))], axis=1)
    kept = moved(slice_out, lambda h, z, c, l: (h, l, c, z))
    copies = copies_of(slice_out)
    row = lax.all_to_all(copies, "dist", split_axis=0, concat_axis=0, tiled=True)
    row = row.reshape(GRID, GRID * GRID)
    crossed = moved(kept, cores)
    seat = lax.axis_index("grp").astype(jnp.int32).reshape(1)
    pair, seat = lax.optimization_barrier((jnp.stack([kept, crossed]), seat))
    live = seat[0] >= 0
    left, right = tables()
    left = jnp.where(live, left, 0)
    right = jnp.where(live, right, 0)
    green = green_table(live)
    hop = {}
    for k in (1, 3, 2):
        hop[k] = moved(pair, ring(k))
    held, first, left, right, green = lax.optimization_barrier((pair, hop[1], left, right, green))
    early = jnp.concatenate([held, first])
    far_early = moved(early, halves)
    core_early = moved(jnp.where(live, first, 0), cores)
    fourth = moved(jnp.where(live, hop[3], 0), ring(1))
    late = jnp.concatenate([hop[3], hop[2]])
    core_late = moved(late, cores)
    far_late = moved(late, halves)
    far_fourth = moved(fourth, halves)
    mine, other = (early, late, fourth), (core_early, core_late)
    partial = solve(seat, row, mine, other, left, right, green)
    far_early, partial = lax.optimization_barrier((far_early, partial))
    swapped = far_early[2:]
    far_core_early = moved(swapped, cores)
    far_late, swapped = lax.optimization_barrier((far_late, swapped))
    far_core_late = moved(far_late, cores)
    mine, other = (far_early, far_late, far_fourth), (far_core_early, far_core_late)
    partial = solve(seat, row, mine, other, left, right, green, partial)
    sent = partial.astype(jnp.float16).reshape(8, 8, GRID * GRID + 128)
    arrived = lax.all_to_all(sent, "dist", split_axis=0, concat_axis=0, tiled=True)
    power = lax.optimization_barrier(arrived[:, 0:1, GRID * GRID : GRID * GRID + 1])
    terms = arrived[:, :, : GRID * GRID].astype(jnp.float32) * jnp.exp2(power.astype(jnp.float32))
    return terms.sum(axis=0)[None]


def solution(mesh):
    in_specs = (P("grp", "dist", None), P("grp"))
    out_specs = P("grp", "dist", None)
    return jax.shard_map(body, mesh=mesh, in_specs=in_specs, out_specs=out_specs, check_vma=False)
```

```python
import functools
import math

import jax
import jax.numpy as jnp
import numpy as np
from jax import lax
from jax.experimental import pallas as pl
from jax.experimental.pallas import tpu as pltpu
from jax.sharding import PartitionSpec as P

GRID = 64
GM = 32
PITCH = 65
box_length = 7.0


def split(x):
    hi = x.astype(jnp.bfloat16)
    lo = (x - hi.astype(jnp.float32)).astype(jnp.bfloat16)
    return hi, lo


def tables():
    position = np.arange(GRID)
    angles = (position[:, None] * position[None, :] % GRID) * (2.0 * math.pi / GRID)
    t = np.cos(angles) + np.sin(angles)
    hi = t.astype(jnp.bfloat16)
    lo = (t - hi.astype(np.float64)).astype(jnp.bfloat16)
    hi, lo = jnp.asarray(hi), jnp.asarray(lo)
    zero = jnp.zeros_like(hi)
    left = jnp.concatenate([jnp.concatenate([hi, hi], 1), jnp.concatenate([lo, zero], 1)], 0)
    two = lambda m: jnp.concatenate([jnp.concatenate([m, zero], 1), jnp.concatenate([zero, m], 1)], 0)
    wide = jnp.concatenate([two(hi), two(lo)], axis=1)
    right = jnp.concatenate([wide, wide], axis=0)
    return left, right


def green_table(live):
    p = jnp.arange(GRID, dtype=jnp.int32)
    f = jnp.minimum(p, GRID - p)
    sq = (f * f).astype(jnp.float32)
    tot = sq[: GRID // 2 + 1, None, None] + sq[None, :, None] + jnp.concatenate([sq, sq])[None, None, :]
    c = jnp.where(live, box_length**2 / (math.pi * GRID**3), 0.0)
    return jnp.where(tot > 0.5, c / jnp.maximum(tot, 1.0), 0.0)


def dot(a, b):
    return jnp.dot(a, b, preferred_element_type=jnp.float32)


def along_lanes(x, right):
    hi, lo = split(x)
    y = dot(jnp.concatenate([hi, lo], axis=1), right)
    return y[:, :128] + y[:, 128:]


def along_rows(left, x):
    hi, lo = split(x)
    y = dot(left, jnp.concatenate([hi, lo], axis=0))
    return y[:GRID] + y[GRID:]


def solve_kernel(first, seat_ref, row_ref, *refs):
    early_ref, late_ref, fourth_ref, other_early_ref, other_late_ref = refs[:5]
    left_ref, right_ref, green_ref = refs[5:8]
    col_ref, f_ref = refs[-2:]
    out_ref = refs[-3]
    group = seat_ref[0]
    core = jnp.bitwise_and(group, 1)
    z = jnp.bitwise_and(jnp.right_shift(group, 1), 7)

    def place(ref, start, holder, block):
        rows = pl.ds(pl.multiple_of(8 * jnp.bitwise_and(block + 8, 7), 8), 8)
        for i in range(2):
            col_ref[jnp.bitwise_xor(i, holder), rows, :] = ref[start + i].astype(jnp.float32)

    place(early_ref, 0, core, z)
    place(fourth_ref, 0, core, z + 4)
    sides = ((core, early_ref, 2, late_ref), (1 - core, other_early_ref, 0, other_late_ref))
    for holder, early, start, late in sides:
        sign = jnp.where(holder == 0, -1, 1)
        place(early, start, holder, z + sign)
        place(late, 0, holder, z + 3 * sign)
        place(late, 2, holder, z + 2 * sign)

    left = left_ref[...]
    right = right_ref[...]
    low = lax.broadcasted_iota(jnp.int32, (GRID, 128), 1) < 64

    packed = []
    for i in range(32):
        lanes = slice(128 * i, 128 * i + 128)
        row = row_ref[:, lanes].astype(jnp.float32)
        d1 = row * col_ref[0, :, lanes]
        d2 = row * col_ref[1, :, lanes]
        packed.append(jnp.where(low, d1, pltpu.roll(d2, 64, 1)))
        packed.append(jnp.where(low, pltpu.roll(d1, 64, 1), d2))
    g = along_lanes(jnp.concatenate(packed, axis=0), right)
    wide = jnp.concatenate([g[64 * i : 64 * i + 64] for i in range(64)], axis=1)
    h = along_rows(left, wide)
    for i in range(64):
        f_ref[PITCH * i : PITCH * i + 64, :] = h[:, 128 * i : 128 * i + 128]

    def middle(step, _):
        kx = step * GM
        parts = [f_ref[pl.ds(kx + i, 64, stride=PITCH), :] for i in range(GM)]
        h = along_rows(left, jnp.concatenate(parts, axis=1))
        folded = [jnp.minimum(kx + i, GRID - kx - i) for i in range(GM)]
        h = h * jnp.concatenate([green_ref[k] for k in folded], axis=1)
        u = along_rows(left, h)
        for i in range(GM):
            f_ref[pl.ds(kx + i, 64, stride=PITCH), :] = u[:, 128 * i : 128 * i + 128]
        return 0

    lax.fori_loop(0, 64 // GM, middle, 0)

    occ = [-col_ref[member, 0:1, 4096:4224] for member in range(2)]
    wide = jnp.concatenate([f_ref[PITCH * i : PITCH * i + 64, :] for i in range(64)], axis=1)
    g = along_rows(left, wide)
    tall = jnp.concatenate([g[:, 128 * i : 128 * i + 128] for i in range(64)], axis=0)
    p = along_lanes(tall, right)
    for i in range(32):
        lanes = slice(128 * i, 128 * i + 128)
        p0, p1 = p[128 * i : 128 * i + 64], p[128 * i + 64 : 128 * i + 128]
        v1 = jnp.where(low, p0, pltpu.roll(p1, 64, 1))
        v2 = jnp.where(low, pltpu.roll(p0, 64, 1), p1)
        term = v1 * (col_ref[0, :, lanes] * occ[0]) + v2 * (col_ref[1, :, lanes] * occ[1])
        if not first:
            term = refs[8][:, lanes] + term
        out_ref[:, lanes] = term

    if not first:
        level = jnp.zeros((GRID, 128), jnp.float32)
        for i in range(32):
            level = jnp.maximum(level, jnp.abs(out_ref[:, 128 * i : 128 * i + 128]))
        peak = jnp.maximum(jnp.max(level, axis=(0, 1), keepdims=True), 1e-30)
        power = jnp.ceil(jnp.log2(jnp.broadcast_to(peak, (8, 128)))) - 15.0
        factor = jnp.exp2(-power)[0:1]
        for i in range(32):
            lanes = slice(128 * i, 128 * i + 128)
            out_ref[:, lanes] = out_ref[:, lanes] * factor
        out_ref[:, 4096:4224] = jnp.broadcast_to(power[0:1], (GRID, 128))


def copies_kernel(x_ref, out_ref, sem):
    source = x_ref.at[:, : GRID * GRID]
    sends = [pltpu.make_async_copy(source, out_ref.at[i], sem.at[i]) for i in range(8)]
    for send in sends:
        send.start()
    for send in sends:
        send.wait()


def copies_of(x):
    return pl.pallas_call(
        copies_kernel,
        out_shape=jax.ShapeDtypeStruct((8, 8, GRID * GRID), x.dtype),
        in_specs=[pl.BlockSpec(memory_space=pltpu.VMEM)],
        out_specs=pl.BlockSpec(memory_space=pl.ANY),
        scratch_shapes=[pltpu.SemaphoreType.DMA((8,))],
        compiler_params=pltpu.CompilerParams(vmem_limit_bytes=2**20),
        name="copies",
    )(x)


def solve(seat, row, mine, other, left, right, green, *more):
    vm = pl.BlockSpec(memory_space=pltpu.VMEM)
    sm = pl.BlockSpec(memory_space=pltpu.SMEM)
    width = GRID * GRID + (128 if more else 0)
    return pl.pallas_call(
        functools.partial(solve_kernel, not more),
        out_shape=jax.ShapeDtypeStruct((GRID, width), jnp.float32),
        in_specs=[sm] + [vm] * (9 + len(more)),
        out_specs=vm,
        scratch_shapes=[
            pltpu.VMEM((2, GRID, GRID * GRID + 128), jnp.float32),
            pltpu.VMEM((GRID * PITCH, 128), jnp.float32),
        ],
        cost_estimate=pl.CostEstimate(flops=10**10, bytes_accessed=10**7, transcendentals=0),
        compiler_params=pltpu.CompilerParams(vmem_limit_bytes=32 * 2**20),
        name="solve",
    )(seat, row, *mine, *other, left, right, green, *more)


AXES = ("grp", "dist")


def device(half, z, core, lane):
    return ((half * 8 + z) * 2 + core) * 8 + lane


def moved(x, rule):
    pairs = [
        (device(h, z, c, l), device(*rule(h, z, c, l)))
        for h in range(2)
        for z in range(8)
        for c in range(2)
        for l in range(8)
    ]
    return lax.ppermute(x, AXES, pairs)


def body(orbitals, occupations):
    return exchange(orbitals[0], occupations[0])


def cores(h, z, c, l):
    return (h, z, 1 - c, l)


def halves(h, z, c, l):
    return (1 - h, z, c, l)


def ring(k):
    return lambda h, z, c, l: (h, (z + (k if c == 0 else 8 - k)) % 8, c, l)


def exchange(mine, occupation):
    slice_out = jnp.concatenate([mine, jnp.broadcast_to(occupation, (8, 128))], axis=1)
    kept = moved(slice_out, lambda h, z, c, l: (h, l, c, z))
    copies = copies_of(slice_out)
    row = lax.all_to_all(copies, "dist", split_axis=0, concat_axis=0, tiled=True)
    row = row.reshape(GRID, GRID * GRID)
    crossed = moved(kept, cores)
    seat = lax.axis_index("grp").astype(jnp.int32).reshape(1)
    pair, seat = lax.optimization_barrier((jnp.stack([kept, crossed]), seat))
    live = seat[0] >= 0
    left, right = tables()
    left = jnp.where(live, left, 0)
    right = jnp.where(live, right, 0)
    green = green_table(live)
    hop = {}
    for k in (1, 3, 2):
        hop[k] = moved(pair, ring(k))
    held, first, left, right, green = lax.optimization_barrier((pair, hop[1], left, right, green))
    early = jnp.concatenate([held, first])
    far_early = moved(early, halves)
    core_early = moved(jnp.where(live, first, 0), cores)
    fourth = moved(jnp.where(live, hop[3], 0), ring(1))
    late = jnp.concatenate([hop[3], hop[2]])
    core_late = moved(late, cores)
    far_late = moved(late, halves)
    far_fourth = moved(fourth, halves)
    mine, other = (early, late, fourth), (core_early, core_late)
    partial = solve(seat, row, mine, other, left, right, green)
    far_early, partial = lax.optimization_barrier((far_early, partial))
    swapped = far_early[2:]
    far_core_early = moved(swapped, cores)
    far_late, swapped = lax.optimization_barrier((far_late, swapped))
    far_core_late = moved(far_late, cores)
    mine, other = (far_early, far_late, far_fourth), (far_core_early, far_core_late)
    partial = solve(seat, row, mine, other, left, right, green, partial)
    sent = partial.astype(jnp.float16).reshape(8, 8, GRID * GRID + 128)
    arrived = lax.all_to_all(sent, "dist", split_axis=0, concat_axis=0, tiled=True)
    power = lax.optimization_barrier(arrived[:, 0:1, GRID * GRID : GRID * GRID + 1])
    terms = arrived[:, :, : GRID * GRID].astype(jnp.float32) * jnp.exp2(power.astype(jnp.float32))
    return terms.sum(axis=0)[None]


def solution(mesh):
    in_specs = (P("grp", "dist", None), P("grp"))
    out_specs = P("grp", "dist", None)
    return jax.shard_map(body, mesh=mesh, in_specs=in_specs, out_specs=out_specs, check_vma=False)
```
